128 devices in a mesh: lat: 8 (over z, core), lon: 16 (over y, x).
Axes of the slice: x: 4, y: 4, z: 4, core: 2. Of those that a mesh axis runs over, the one named last changes fastest.
Arguments:
- east_courant: float32 [2, 16, 768, 2048], P(None, None, 'lat', 'lon'), may hold values from 0.3 to 400
- north_courant: float32 [2, 16, 768, 2048], P(None, None, 'lat', 'lon'), may hold values from -0.45 to 0.45
- kernels: float32 [2, 16, 131072], P(None, None, ('lat', 'lon')), may hold values from 0.1 to 1.2
- departures: float32 [2, 2, 131072], P(None, None, ('lat', 'lon')), may hold values from -6 to 6
- cells: int32 [2, 131072], P(None, ('lat', 'lon')), may hold values from 0 to 12287
- counts: int32 [2, 16384], P(None, ('lat', 'lon')), may hold values from 1 to 8, as said below
Outputs:
- adjoint_state: float32 [2, 16, 768, 2048], P(None, None, 'lat', 'lon')
- flux_gradient: float32 [2, 768, 2048], P(None, 'lat', 'lon')
The draws below stay inside these ranges and needn't reach their ends.
Inputs may be any that keep to these rules, and one draw needn't show every extreme that they name: counts[n, s * 128 + o] is the number of live slots from device s to owner o in step n; in every step some owner receives 8 from every device. `cells`: a cell of the owner's block, row-major over 96 x 128.
All inputs are finite; a program needn't handle non-finite values.
Results may differ from the reference program's by a relative error of at most 0.0003.
Values sent between devices are 32-bit elements; how exact they have to be, the bound alone decides.
No kernel may reach another device: no remote copies, remote signals or barrier semaphores. Data moves between devices by JAX's collectives and lax.ppermute only.
A program may use at most 192 MiB of HBM per device.

```python
import math
import jax
import jax.numpy as jnp
from jax import lax

TR = 2
LEV = 16
CLAT = 96
CLON = 128
STEPS = 2
CAP = 8
OWNERS = 128
NLAT = 768
NLON = 2048
SLOTS = 131072
N_LON = 16


def draw_east_courant(key, part):
    unit_draw = jax.random.uniform(key, (STEPS, LEV, NLAT, NLON), jnp.float32)
    low_log = math.log(0.301)
    high_log = math.log(60.0)
    return jnp.exp(low_log + (high_log - low_log) * unit_draw)


def draw_departures(key, part):
    noise = jax.random.normal(key, (STEPS, TR, SLOTS), jnp.float32)
    value_draw = noise
    return jnp.clip(value_draw, -6.0, 6.0)


def draw_counts(key, part):
    key_busy, key_quiet, key_heavy, key_full = jax.random.split(key, 4)
    busy_owner = jax.random.randint(key_busy, (STEPS, 1, OWNERS), 0, 4) == 0
    quiet_draw = jax.random.randint(key_quiet, (STEPS, OWNERS, OWNERS), 1, CAP // 2 + 1)
    heavy_draw = jax.random.randint(key_heavy, (STEPS, OWNERS, OWNERS), CAP // 2, CAP + 1)
    full_owner = jax.random.randint(key_full, (STEPS, 1, 1), 0, OWNERS)
    destination = lax.broadcasted_iota(jnp.int32, (STEPS, OWNERS, OWNERS), 2)
    count_draw = jnp.where(busy_owner, heavy_draw, quiet_draw)
    count_draw = jnp.where(destination == full_owner, CAP, count_draw)
    return count_draw.reshape(STEPS, OWNERS * OWNERS).astype(jnp.int32)


def place_ends(result, rng, low, high):
    longest = result.shape.index(max(result.shape))
    spots = []
    for shift in (0, 1):
        where = [jax.random.randint(jax.random.fold_in(rng, axis), (), 0, length) for axis, length in enumerate(result.shape)]
        where[longest] = (where[longest] + shift) % result.shape[longest]
        spots.append(tuple(where))
    return result.at[spots[0]].set(low).at[spots[1]].set(high)


def block_scale(stream_key, extent, cuts, low, high):
    factor_of = 1.0
    for position, shards_of in cuts:
        heights = jax.random.uniform(jax.random.fold_in(jax.random.fold_in(stream_key, 6), position), (shards_of,), jnp.float32, low / len(cuts), high / len(cuts))
        factor_of = factor_of * jnp.repeat(jnp.exp(heights), extent[position] // shards_of).reshape((-1,) + (1,) * (len(extent) - 1 - position))
    return factor_of


def setup_inputs(seed: int = 0) -> dict:
    key_of = jax.random.split(jax.random.key(seed), 7)
    east_courant = draw_east_courant(jax.random.fold_in(key_of[6], 71), 0)
    north_courant = jnp.clip(jax.random.uniform(key_of[1], (STEPS, LEV, NLAT, NLON), jnp.float32, -0.45, 0.45) * block_scale(key_of[1], (STEPS, LEV, NLAT, NLON), ((2, 8), (3, 16)), -0.4, 0.0), -0.45, 0.45)
    kernels = jnp.clip(0.1 + 1.1 * jax.random.uniform(key_of[2], (STEPS, LEV, SLOTS), jnp.float32) ** block_scale(key_of[2], (STEPS, LEV, SLOTS), ((2, 128),), -0.2, 0.2), 0.1, 1.2)
    departures = draw_departures(jax.random.fold_in(key_of[6], 71), 0)
    cells = place_ends(jax.random.randint(key_of[4], (STEPS, SLOTS), 0, CLAT * CLON), jax.random.fold_in(key_of[4], 1), 0, (CLAT * CLON) - 1).astype(jnp.int32)
    counts = draw_counts(jax.random.fold_in(key_of[6], 71), 0)
    return dict(east_courant=east_courant, north_courant=north_courant, kernels=kernels, departures=departures, cells=cells, counts=counts)


def compose(outer_map, inner_map):
    return (outer_map[0] * inner_map[0], outer_map[0] * inner_map[1] + outer_map[1])


def reverse_pair(higher, lower_map):
    return compose(lower_map, higher)


def cyclic_solve(retain, source, along):
    affine = lax.associative_scan(reverse_pair, (retain, source), reverse=True, axis=along)
    first_gain = lax.slice_in_dim(affine[0], 0, 1, axis=along)
    first_rest = lax.slice_in_dim(affine[1], 0, 1, axis=along)
    closure = first_rest / (1.0 - first_gain)
    return affine[0] * closure + affine[1]


def forcing(kernels, departures, cells, counts):
    slot_index = jnp.arange(SLOTS, dtype=jnp.int32)
    per_source = OWNERS * CAP
    source = slot_index // per_source
    owner = (slot_index % per_source) // CAP
    within = slot_index % CAP
    live_slot = within < counts[source * OWNERS + owner]
    lat_cell = (owner // N_LON) * CLAT + cells // CLON
    lon_cell = (owner % N_LON) * CLON + cells % CLON
    flat_cell = (lat_cell * NLON + lon_cell).astype(jnp.int32)
    values = departures * live_slot.astype(departures.dtype)
    terms = values[:, None, :] * kernels[None, :, :]
    field = jnp.zeros((TR, LEV, NLAT * NLON), jnp.float32).at[:, :, flat_cell].add(terms)
    return field.reshape(TR, LEV, NLAT, NLON)


def lat_adjoint(adjoint, north):
    lat_rows = north.shape[1]
    top_row = lax.broadcasted_iota(jnp.int32, north.shape, 1) == lat_rows - 1
    north_faces = jnp.where(top_row, 0.0, north)
    northward = jnp.maximum(north_faces, 0.0)
    southward = jnp.minimum(north_faces, 0.0)
    padded = jnp.pad(adjoint, ((0, 0), (0, 0), (1, 1), (0, 0)))
    upper_row = padded[:, :, 2:]
    lower_row = padded[:, :, :-2]
    south_faces = jnp.pad(southward, ((0, 0), (1, 0), (0, 0)))[:, :-1]
    return adjoint + northward * (upper_row - adjoint) + south_faces * (adjoint - lower_row)


def lon_adjoint(adjoint, east):
    retain = east / (1.0 + east)
    weight = 1.0 / (1.0 + east)

    def one_level(inputs):
        level_state, level_retain, level_weight = inputs
        return cyclic_solve(jnp.broadcast_to(level_retain, level_state.shape), level_weight * level_state, 2)

    moved = lax.map(one_level, (jnp.swapaxes(adjoint, 0, 1), retain, weight))
    return jnp.swapaxes(moved, 0, 1)


def reference(east_courant, north_courant, kernels, departures, cells, counts):
    adjoint = jnp.zeros((TR, LEV, NLAT, NLON), jnp.float32)
    flux_gradient = jnp.zeros((TR, NLAT, NLON), jnp.float32)
    for window_step in range(STEPS - 1, -1, -1):
        adjoint = adjoint + forcing(kernels[window_step], departures[window_step], cells[window_step], counts[window_step])
        flux_gradient = flux_gradient + adjoint[:, 0]
        adjoint = lat_adjoint(adjoint, north_courant[window_step])
        adjoint = lon_adjoint(adjoint, east_courant[window_step])
    return adjoint, flux_gradient
```

```python
import jax
import jax.numpy as jnp
from jax import lax
from jax.experimental import pallas as pl
from jax.experimental.pallas import tpu as pltpu
from jax.sharding import PartitionSpec as P

F32 = jnp.float32
BF16 = jnp.bfloat16
STEPS, TR, LEV, ROWS, COLS = 2, 2, 16, 96, 128
SLOTS = 1024
N_LAT, N_LON = 8, 16
PAD = 112
TOP = 8
END = TOP + ROWS
HALF = ROWS // 2
FIELDS = 40
COEF = 5 * LEV
REST = 4 * LEV
VMEM_BYTES = 48 * 1024 * 1024


def iota(shape, dim):
    return lax.broadcasted_iota(jnp.int32, shape, dim)


def ahead(x, k):
    return pltpu.roll(x, COLS - k, 1)


def ladder(retain):
    steps = []
    product = jnp.where(iota(retain.shape, 1) == COLS - 1, 0.0, retain)
    k = 1
    while k < COLS:
        steps.append((k, product))
        if 2 * k < COLS:
            product = product * ahead(product, k)
        k *= 2
    return steps


def solve(steps, source):
    for k, product in steps:
        source = source + product * ahead(source, k)
    return source


def end_gain(steps, retain):
    return solve(steps, jnp.where(iota(retain.shape, 1) == COLS - 1, retain, 0.0))


def lane_value(x, lane):
    return jnp.sum(jnp.where(iota(x.shape, 1) == lane, x, 0.0), axis=1, keepdims=True)


def masked_north(v, is_top):
    return jnp.where((iota(v.shape, 0) == ROWS - 1) & is_top, 0.0, v)


def top_flag():
    return lax.axis_index("lat") == N_LAT - 1


def pack_kernel(ker_ref, dep_ref, cell_ref, cnt_ref, nlast_ref, nfirst_ref, elast_ref, efirst_ref,
                send_ref, up_ref, dn_ref, x_ref):
    for n in range(STEPS):
        x_ref[n * LEV:(n + 1) * LEV, :] = ker_ref[n]
    spread = jnp.where(iota((128, SLOTS), 1) // 8 == iota((128, SLOTS), 0), 1.0, 0.0).astype(BF16)
    counts = jnp.concatenate([cnt_ref[...].astype(F32), jnp.zeros((6, 128), F32)], axis=0)
    counts = jnp.dot(counts.astype(BF16), spread, preferred_element_type=F32)
    within = (iota((8, SLOTS), 1) % 8).astype(F32)
    live = jnp.where(within < counts, 1.0, 0.0)
    rows = []
    for n in range(STEPS):
        rows.append(dep_ref[n] * live[n:n + 1])
    rows.append(cell_ref[...].astype(F32))
    rows.append(jnp.zeros((2, SLOTS), F32))
    x_ref[2 * LEV:FIELDS, :] = jnp.concatenate(rows, axis=0)
    none = jnp.zeros((FIELDS, 128), F32)

    def lanes(b):
        if b < 0 or b >= N_LAT:
            return none
        return x_ref[:, b * 128:(b + 1) * 128]

    for b in range(N_LAT):
        tile = jnp.concatenate([lanes(b), lanes(b - 1), lanes(b + 1), jnp.zeros((8, 128), F32)], axis=0)
        send_ref[b * 128:(b + 1) * 128, :] = tile.T
    up_ref[0] = nlast_ref[0, :, 7, :]
    up_ref[1] = nlast_ref[1, :, 6, :]
    up_ref[2] = nlast_ref[1, :, 7, :]
    up_ref[3] = elast_ref[0, :, 7, :]
    dn_ref[0] = nfirst_ref[0, :, 0, :]
    dn_ref[1] = efirst_ref[0, :, 0, :]


def coef_kernel(east_ref, north_ref, up_ref, dn_ref, gain_ref, w0_ref, q_ref, v_ref, col_ref):
    is_top = top_flag()
    edge_gain = []
    for row, courant in ((TOP - 1, up_ref[3]), (END, dn_ref[1])):
        retain = courant / (1.0 + courant)
        g = end_gain(ladder(retain), retain)
        edge_gain.append(g)
        for lev in range(LEV):
            gain_ref[lev, row:row + 1, :] = g[lev:lev + 1, :]
            if row < TOP:
                v_ref[lev, row:row + 1, :] = up_ref[0, lev:lev + 1, :]
    col_ref[...] = jnp.zeros((128, 128), F32)

    def level(lev, carry):
        lane = iota((ROWS, COLS), 1)
        c1 = east_ref[1, lev]
        r1 = c1 / (1.0 + c1)
        g1 = end_gain(ladder(r1), r1)
        gain_ref[lev, TOP:END, :] = g1
        w0 = 1.0 / (1.0 + east_ref[0, lev])
        r0 = east_ref[0, lev] * w0
        before = jnp.where(lane == 0, 1.0, pltpu.roll(r0, 1, 1))
        k = 1
        while k < COLS:
            before = before * jnp.where(lane >= k, pltpu.roll(before, k, 1), 1.0)
            k *= 2
        weight = w0 * before
        w0_ref[lev] = weight
        v = masked_north(north_ref[0, lev], is_top)
        v_ref[lev, TOP:END, :] = v
        north = jnp.maximum(v, 0.0)
        south = jnp.minimum(v_ref[lev, TOP - 1:END - 1, :], 0.0)
        here = jnp.sum(weight * (1.0 - north + south) * g1, axis=1, keepdims=True)
        upper = jnp.sum(weight * north * gain_ref[lev, TOP + 1:END + 1, :], axis=1, keepdims=True)
        lower = jnp.sum(-weight * south * gain_ref[lev, TOP - 1:END - 1, :], axis=1, keepdims=True)
        block1 = lane_value(g1, 0)
        block0 = lane_value(before * r0, COLS - 1)
        col = col_ref[0:ROWS, :]
        for i, value in enumerate((block1, here, upper, lower, block0)):
            col = jnp.where(lane == lev + i * LEV, value, col)
        col_ref[0:ROWS, :] = col
        return carry

    lax.fori_loop(0, LEV, level, 0)
    q = col_ref[...].T
    lane = iota((LEV, 128), 1)
    q_ref[...] = q[0:COEF]
    first = jnp.where(lane == ROWS, lane_value(edge_gain[1], 0), q[0:LEV])
    q_ref[0:LEV, :] = jnp.where(lane == 127, lane_value(edge_gain[0], 0), first)


def split(x):
    high = x.astype(BF16).astype(F32)
    return high, x - high


def product_nt(a, b):
    return lax.dot_general(a, b, (((1,), (1,)), ((), ())), preferred_element_type=F32)


def state_kernel(recv_ref, east_ref, north_ref, up_ref, dn_ref, w0_ref, q1_ref,
                 send_ref, b_ref, flux_ref,
                 x_ref, f_ref, v1_ref, v0_ref, col_ref, term_ref, lhs_ref, rhs_ref, mask_ref):
    is_top = top_flag()
    for b in range(N_LAT):
        x_ref[:, b * 128:(b + 1) * 128] = recv_ref[b * 128:(b + 1) * 128, :].T

    def place(offset, n):
        cell = x_ref[offset + 36 + n:offset + 37 + n, :].astype(jnp.int32)
        return cell >> 7, cell & 127

    def make_terms(offset, n):
        parts = []
        for t in range(TR):
            value = x_ref[offset + 32 + 2 * n + t:offset + 33 + 2 * n + t, :]
            parts.append(split(value * x_ref[offset + n * LEV:offset + (n + 1) * LEV, :]))
        return parts

    group = 4
    for n in (1, 0):
        target = f_ref if n else b_ref
        parts = make_terms(0, n)
        for t in range(TR):
            for p in range(2):
                term_ref[t, p] = parts[t][p]
        row, col = place(0, n)
        later = row >= HALF
        row = jnp.where(later, row - HALF, row)
        col = jnp.where(later, col + COLS, col)
        mask_ref[...] = jnp.where(iota((HALF, SLOTS), 0) == row, 1.0, 0.0)
        rhs_ref[...] = jnp.where(iota((2 * COLS, SLOTS), 0) == col, 1.0, 0.0).astype(BF16)

        def levels(g, carry, target=target):
            for i in range(group):
                for t in range(TR):
                    for p in range(2):
                        at = ((i * TR + t) * 2 + p) * HALF
                        term = term_ref[t, p, pl.ds(g * group + i, 1), :]
                        lhs_ref[at:at + HALF, :] = (mask_ref[...] * term).astype(BF16)
            out = product_nt(lhs_ref[...], rhs_ref[...])
            for i in range(group):
                for t in range(TR):
                    at = (i * TR + t) * 2 * HALF
                    both = out[at:at + HALF] + out[at + HALF:at + 2 * HALF]
                    target[t * LEV + g * group + i, TOP:TOP + HALF, :] = both[:, :COLS]
                    target[t * LEV + g * group + i, TOP + HALF:END, :] = both[:, COLS:]
            return carry

        lax.fori_loop(0, LEV // group, levels, 0)

    edges = {}
    for side, offset in ((0, FIELDS), (1, 2 * FIELDS)):
        for n in (1, 0):
            rows = ((ROWS - 1, ROWS - 2), (0, 1))[side][:2 if n else 1]
            row, col = place(offset, n)
            hot = jnp.where(iota((COLS, SLOTS), 0) == col, 1.0, 0.0).astype(BF16)
            parts = make_terms(offset, n)
            stack = []
            for r in rows:
                hit = jnp.where(row == r, 1.0, 0.0)
                for t in range(TR):
                    for p in range(2):
                        stack.append((parts[t][p] * hit).astype(BF16))
            out = product_nt(jnp.concatenate(stack, axis=0), hot)
            for i in range(len(rows)):
                for t in range(TR):
                    at = (i * TR + t) * 2 * LEV
                    edges[side, n, i, t] = out[at:at + LEV] + out[at + LEV:at + 2 * LEV]

    edge_rest = {}
    for side in range(2):
        courant = (up_ref[3], dn_ref[1])[side]
        weight = 1.0 / (1.0 + courant)
        steps = ladder(courant * weight)
        for t in range(TR):
            near = edges[side, 1, 0, t]
            far = edges[side, 1, 1, t]
            inner = f_ref[t * LEV:(t + 1) * LEV, TOP if side == 0 else END - 1, :]
            if side == 0:
                north = jnp.maximum(up_ref[2], 0.0)
                south = jnp.minimum(up_ref[1], 0.0)
                y = near + north * (inner - near) + south * (near - far)
            else:
                north = jnp.maximum(dn_ref[0], 0.0)
                south = jnp.minimum(jnp.where(is_top, 0.0, north_ref[1, :, ROWS - 1, :]), 0.0)
                y = near + north * (far - near) + south * (near - inner)
            rest = solve(steps, weight * y)
            edge_rest[side, t] = lane_value(rest, 0)
            at = TOP - 1 if side == 0 else END
            total = rest + edges[side, 0, 0, t]
            for lev in range(LEV):
                b_ref[t * LEV + lev, at:at + 1, :] = total[lev:lev + 1, :]
                f_ref[t * LEV + lev, at:at + 1, :] = near[lev:lev + 1, :]
    for lev in range(LEV):
        v1_ref[lev, TOP - 1:TOP, :] = up_ref[2, lev:lev + 1, :]
        v0_ref[lev, TOP - 1:TOP, :] = up_ref[0, lev:lev + 1, :]
    for t in range(TR):
        flux_ref[t] = f_ref[t * LEV, TOP:END, :]
    col_ref[...] = jnp.zeros((128, 128), F32)

    def level(lev, carry):
        lane = iota((ROWS, COLS), 1)
        courant = east_ref[0, lev]
        weight = 1.0 / (1.0 + courant)
        steps = ladder(courant * weight)
        v1 = masked_north(north_ref[1, lev], is_top)
        v1_ref[lev, TOP:END, :] = v1
        north1 = jnp.maximum(v1, 0.0)
        south1 = jnp.minimum(v1_ref[lev, TOP - 1:END - 1, :], 0.0)
        v0 = masked_north(north_ref[0, lev], is_top)
        v0_ref[lev, TOP:END, :] = v0
        north0 = jnp.maximum(v0, 0.0)
        south0 = jnp.minimum(v0_ref[lev, TOP - 1:END - 1, :], 0.0)
        weight0 = w0_ref[lev]
        col = col_ref[0:ROWS, :]
        for t in range(TR):
            at = t * LEV + lev
            a = f_ref[at, TOP:END, :]
            y = a + north1 * (f_ref[at, TOP + 1:END + 1, :] - a) + south1 * (a - f_ref[at, TOP - 1:END - 1, :])
            rest = solve(steps, weight * y)
            col = jnp.where(lane == lev + t * LEV, lane_value(rest, 0), col)
            a = b_ref[at, TOP:END, :] + rest
            b_ref[at, TOP:END, :] = a
            y = a + north0 * (b_ref[at, TOP + 1:END + 1, :] - a) + south0 * (a - b_ref[at, TOP - 1:END - 1, :])
            value = jnp.sum(weight0 * y, axis=1, keepdims=True)
            col = jnp.where(lane == lev + (TR + t) * LEV, value, col)
        col_ref[0:ROWS, :] = col
        return carry

    lax.fori_loop(0, LEV, level, 0)
    q = col_ref[...].T
    lane = iota((LEV, 128), 1)
    tiles = []
    for t in range(TR):
        first = jnp.where(lane == ROWS, edge_rest[1, t], q[t * LEV:(t + 1) * LEV])
        tiles.append(jnp.where(lane == 127, edge_rest[0, t], first))
    tiles.append(q[TR * LEV:2 * TR * LEV])
    q2 = jnp.concatenate(tiles, axis=0)
    q1 = q1_ref[...]
    for j in range(N_LON):
        send_ref[j, 0:REST, :] = q2
        send_ref[j, REST:, :] = q1


def final_kernel(recv_ref, b_ref, gain_ref, east_ref, north_ref, up_ref, f1_ref,
                 adj_ref, flux_ref, in1_ref, in0_ref, c_ref, v_ref, a_ref):
    is_top = top_flag()
    me = lax.axis_index("lon")

    def part(j, i, width=1):
        return recv_ref[j, i * LEV:(i + width) * LEV, :]

    for t in range(TR):
        gain = jnp.ones((LEV, 128), F32)
        rest = jnp.zeros((LEV, 128), F32)
        for j in range(N_LON - 1, -1, -1):
            g = part(j, 4)
            rest = g * rest + part(j, t)
            gain = g * gain
        inflow = rest / (1.0 - gain)
        gain = jnp.ones((LEV, 128), F32)
        rest = jnp.zeros((LEV, 128), F32)
        for j in range(N_LON - 1, -1, -1):
            in1_ref[j, t * LEV:(t + 1) * LEV, :] = inflow
            total = part(j, TR + t) + part(j, 5) * inflow
            total = total + part(j, 6) * ahead(inflow, 1) + part(j, 7) * pltpu.roll(inflow, 1, 1)
            in0_ref[j, t * LEV:(t + 1) * LEV, :] = total
            inflow = part(j, 4) * inflow + part(j, t)
            g = part(j, 8)
            rest = g * rest + total
            gain = g * gain
        inflow = rest / (1.0 - gain)
        for j in range(N_LON - 1, -1, -1):
            total = in0_ref[j, t * LEV:(t + 1) * LEV, :]
            in0_ref[j, t * LEV:(t + 1) * LEV, :] = inflow
            inflow = part(j, 8) * inflow + total
    in1 = in1_ref[me]
    in0 = in0_ref[me]
    c_ref[...] = jnp.concatenate([in1, in0, jnp.zeros((64, 128), F32)], axis=0).T
    for side, row in ((0, TOP - 1), (1, END)):
        for t in range(TR):
            flow = lane_value(in1[t * LEV:(t + 1) * LEV], (127, ROWS)[side])
            for lev in range(LEV):
                at = t * LEV + lev
                a_ref[at, row:row + 1, :] = b_ref[at, row:row + 1, :] + gain_ref[lev, row:row + 1, :] * flow[lev:lev + 1]
    for lev in range(LEV):
        v_ref[lev, TOP - 1:TOP, :] = up_ref[0, lev:lev + 1, :]

    def level(lev, carry):
        courant = east_ref[0, lev]
        weight = 1.0 / (1.0 + courant)
        retain = courant * weight
        steps = ladder(retain)
        gain0 = end_gain(steps, retain)
        v = masked_north(north_ref[0, lev], is_top)
        v_ref[lev, TOP:END, :] = v
        north = jnp.maximum(v, 0.0)
        south = jnp.minimum(v_ref[lev, TOP - 1:END - 1, :], 0.0)
        gain1 = gain_ref[lev, TOP:END, :]
        flows = pltpu.roll(c_ref[...], 128 - lev, 1)[0:ROWS]
        for t in range(TR):
            at = t * LEV + lev
            a = b_ref[at, TOP:END, :] + gain1 * flows[:, t * LEV:t * LEV + 1]
            a_ref[at, TOP:END, :] = a
            y = a + north * (a_ref[at, TOP + 1:END + 1, :] - a) + south * (a - a_ref[at, TOP - 1:END - 1, :])
            u = solve(steps, weight * y)
            adj_ref[t, lev] = u + gain0 * flows[:, (TR + t) * LEV:(TR + t) * LEV + 1]
        return carry

    lax.fori_loop(0, LEV, level, 0)
    for t in range(TR):
        flux_ref[t] = f1_ref[t] + a_ref[t * LEV, TOP:END, :]


def spec(block, index):
    return pl.BlockSpec(block, lambda i: index)


def whole(shape):
    return pl.BlockSpec(shape, lambda i: (0,) * len(shape))


def call(kernel, outs, in_specs, scratch, name):
    return pl.pallas_call(
        kernel,
        out_shape=[jax.ShapeDtypeStruct(s, F32) for s in outs],
        grid=(1,),
        in_specs=in_specs,
        out_specs=[whole(s) for s in outs],
        scratch_shapes=[pltpu.VMEM(s, d) for s, d in scratch],
        compiler_params=pltpu.CompilerParams(vmem_limit_bytes=VMEM_BYTES),
        name=name,
    )


def shards(east, north, kernels, departures, cells, counts):
    edge = (2, LEV, 8, COLS)
    one = (1, LEV, 8, COLS)
    last = ROWS // 8 - 1
    send, up, dn = call(
        pack_kernel,
        [(SLOTS, 128), (4, LEV, COLS), (2, LEV, COLS)],
        [whole(kernels.shape), whole(departures.shape), whole(cells.shape), whole(counts.shape),
         spec(edge, (0, 0, last, 0)), spec(one, (1, 0, 0, 0)), spec(one, (1, 0, last, 0)), spec(one, (1, 0, 0, 0))],
        [((FIELDS, SLOTS), F32)],
        "pack",
    )(kernels, departures, cells, counts, north, north, east, east)
    recv = lax.all_to_all(send.reshape(128, 8, 128), ("lat", "lon"), split_axis=0, concat_axis=0, tiled=True)
    up = lax.ppermute(up, "lat", [(i, i + 1) for i in range(N_LAT - 1)])
    dn = lax.ppermute(dn, "lat", [(i + 1, i) for i in range(N_LAT - 1)])
    field = (STEPS, LEV, ROWS, COLS)
    half = (1, LEV, ROWS, COLS)
    gain, w0, q1 = call(
        coef_kernel,
        [(LEV, PAD, COLS), (LEV, ROWS, COLS), (COEF, 128)],
        [whole(field), spec(half, (0, 0, 0, 0)), whole(up.shape), whole(dn.shape)],
        [((LEV, PAD, COLS), F32), ((128, 128), F32)],
        "coef",
    )(east, north, up, dn)
    send2, b, f1 = call(
        state_kernel,
        [(N_LON, REST + COEF, 128), (TR * LEV, PAD, COLS), (TR, ROWS, COLS)],
        [whole((SLOTS, 128)), spec(half, (1, 0, 0, 0)), whole(field), whole(up.shape), whole(dn.shape),
         whole(w0.shape), whole(q1.shape)],
        [((128, SLOTS), F32), ((TR * LEV, PAD, COLS), F32), ((LEV, PAD, COLS), F32), ((LEV, PAD, COLS), F32),
         ((128, 128), F32), ((TR, 2, LEV, SLOTS), F32), ((16 * HALF, SLOTS), BF16), ((2 * COLS, SLOTS), BF16),
         ((HALF, SLOTS), F32)],
        "state",
    )(recv.reshape(SLOTS, 128), east, north, up, dn, w0, q1)
    recv2 = lax.all_to_all(send2, "lon", split_axis=0, concat_axis=0, tiled=True)
    adjoint, flux = call(
        final_kernel,
        [(TR, LEV, ROWS, COLS), (TR, ROWS, COLS)],
        [whole(recv2.shape), whole(b.shape), whole(gain.shape), spec(half, (0, 0, 0, 0)), spec(half, (0, 0, 0, 0)),
         whole(up.shape), whole(f1.shape)],
        [((N_LON, TR * LEV, 128), F32), ((N_LON, TR * LEV, 128), F32), ((128, 128), F32), ((LEV, PAD, COLS), F32),
         ((TR * LEV, PAD, COLS), F32)],
        "final",
    )(recv2, b, gain, east, north, up, f1)
    return adjoint, flux


def solution(mesh):
    return jax.shard_map(
        shards,
        mesh=mesh,
        in_specs=(
            P(None, None, "lat", "lon"),
            P(None, None, "lat", "lon"),
            P(None, None, ("lat", "lon")),
            P(None, None, ("lat", "lon")),
            P(None, ("lat", "lon")),
            P(None, ("lat", "lon")),
        ),
        out_specs=(P(None, None, "lat", "lon"), P(None, "lat", "lon")),
        check_vma=False,
    )
```

```python
import jax
import jax.numpy as jnp
from jax import lax
from jax.experimental import pallas as pl
from jax.experimental.pallas import tpu as pltpu
from jax.sharding import PartitionSpec as P

F32 = jnp.float32
BF16 = jnp.bfloat16
STEPS, TR, LEV, ROWS, COLS = 2, 2, 16, 96, 128
SLOTS = 1024
N_LAT, N_LON = 8, 16
PAD = 112
TOP = 8
END = TOP + ROWS
HALF = ROWS // 2
FIELDS = 40
COEF = 5 * LEV
REST = 4 * LEV
GROUP = 2
CHUNK = 16
MEGA = 1024 * 1024


def iota(shape, dim):
    return lax.broadcasted_iota(jnp.int32, shape, dim)


def row_ahead(x):
    return pltpu.roll(x, 127, 1)


def row_behind(x):
    return pltpu.roll(x, 1, 1)


def chunk_ahead(x, k):
    return pltpu.roll(x, 8 - k, 0)


def load_columns(ref):
    return [ref[pl.ds(m, 8, stride=CHUNK), :] for m in range(CHUNK)]


def load_registers(ref, lead):
    return [ref[lead, 8 * m:8 * m + 8, :] for m in range(CHUNK)]


def store_registers(ref, lead, values):
    for m in range(CHUNK):
        ref[lead, 8 * m:8 * m + 8, :] = values[m]


def suffix(values, retain):
    out = [None] * CHUNK
    out[-1] = values[-1]
    for m in range(CHUNK - 2, -1, -1):
        out[m] = values[m] + retain[m] * out[m + 1]
    return out


def suffix_product(retain):
    out = [None] * CHUNK
    out[-1] = retain[-1]
    for m in range(CHUNK - 2, -1, -1):
        out[m] = retain[m] * out[m + 1]
    return out


def chunk_ladder(product):
    last = iota(product.shape, 0) == 7
    steps = []
    value = jnp.where(last, 0.0, chunk_ahead(product, 1))
    for k in (1, 2, 4):
        steps.append((k, value))
        if k < 4:
            value = value * chunk_ahead(value, k)
    return steps


def chunk_inflow(steps, first, inflow):
    value = jnp.where(iota(first.shape, 0) == 7, inflow, chunk_ahead(first, 1))
    for k, product in steps:
        value = value + product * chunk_ahead(value, k)
    return value


def masked_north(v, is_top):
    return jnp.where((iota(v.shape, 0) == ROWS - 1) & is_top, 0.0, v)


def top_flag():
    return lax.axis_index("lat") == N_LAT - 1


def pack_kernel(ker_hbm, dep_hbm, cell_hbm, cnt_hbm, north_hbm, east_hbm,
                send_ref, up_ref, dn_ref,
                ker_ref, dep_ref, cell_ref, cnt_ref, nlast_ref, nfirst_ref, elast_ref, efirst_ref, x_ref, sems):
    copies = [
        pltpu.make_async_copy(cnt_hbm, cnt_ref, sems.at[0]),
        pltpu.make_async_copy(dep_hbm, dep_ref, sems.at[1]),
        pltpu.make_async_copy(cell_hbm, cell_ref, sems.at[2]),
        pltpu.make_async_copy(ker_hbm, ker_ref, sems.at[3]),
        pltpu.make_async_copy(north_hbm.at[:, :, ROWS - 8:, :], nlast_ref, sems.at[4]),
        pltpu.make_async_copy(north_hbm.at[1, :, :8, :], nfirst_ref, sems.at[5]),
        pltpu.make_async_copy(east_hbm.at[1, :, ROWS - 8:, :], elast_ref, sems.at[6]),
        pltpu.make_async_copy(east_hbm.at[1, :, :8, :], efirst_ref, sems.at[7]),
    ]
    for copy in copies:
        copy.start()
    spread = jnp.where(iota((128, SLOTS), 1) // 8 == iota((128, SLOTS), 0), 1.0, 0.0).astype(BF16)
    within = (iota((8, SLOTS), 1) % 8).astype(F32)
    for copy in copies:
        copy.wait()
    for n in range(STEPS):
        x_ref[n * LEV:(n + 1) * LEV, :] = ker_ref[n]
    counts = jnp.concatenate([cnt_ref[...].astype(F32), jnp.zeros((6, 128), F32)], axis=0)
    counts = jnp.dot(counts.astype(BF16), spread, preferred_element_type=F32)
    live = jnp.where(within < counts, 1.0, 0.0)
    rows = []
    for n in range(STEPS):
        rows.append(dep_ref[n] * live[n:n + 1])
    rows.append(cell_ref[...].astype(F32))
    rows.append(jnp.zeros((2, SLOTS), F32))
    x_ref[2 * LEV:FIELDS, :] = jnp.concatenate(rows, axis=0)
    none = jnp.zeros((FIELDS, 128), F32)

    def lanes(b):
        if b < 0 or b >= N_LAT:
            return none
        return x_ref[:, b * 128:(b + 1) * 128]

    for b in range(N_LAT):
        tile = jnp.concatenate([lanes(b), lanes(b - 1), lanes(b + 1), jnp.zeros((8, 128), F32)], axis=0)
        send_ref[b * 128:(b + 1) * 128, :] = tile.T
    up_ref[0] = nlast_ref[0, :, 7, :]
    up_ref[1] = nlast_ref[1, :, 6, :]
    up_ref[2] = nlast_ref[1, :, 7, :]
    up_ref[3] = elast_ref[:, 7, :]
    dn_ref[0] = nfirst_ref[:, 0, :]
    dn_ref[1] = efirst_ref[:, 0, :]


def coef_kernel(east_ref, north_ref, up_ref, dn_ref,
                w1_ref, w0_ref, north0_ref, south0_ref, here_ref, upper_ref, lower_ref, gain_ref, q_ref,
                he_ref, hv_ref, t_ref):
    is_top = top_flag()
    group = pl.program_id(0)

    @pl.when(group == 0)
    def _():
        he_ref[...] = jnp.zeros(he_ref.shape, F32)
        hv_ref[...] = jnp.zeros(hv_ref.shape, F32)
        for lev in range(LEV):
            he_ref[lev, 0:1, :] = dn_ref[1, lev:lev + 1, :]
            he_ref[lev, 31:32, :] = up_ref[3, lev:lev + 1, :]
            hv_ref[lev, 31:32, :] = up_ref[0, lev:lev + 1, :]

    def level(i, carry):
        lev = group * GROUP + i
        t_ref[0] = jnp.concatenate([east_ref[1, lev], he_ref[lev]], axis=0).T
        t_ref[1] = jnp.concatenate([east_ref[0, lev], jnp.zeros((32, COLS), F32)], axis=0).T
        t_ref[2] = jnp.concatenate([masked_north(north_ref[0, lev], is_top), hv_ref[lev]], axis=0).T
        one = jnp.ones((8, 128), F32)
        none = jnp.zeros((8, 128), F32)
        w1 = [1.0 / (1.0 + c) for c in load_columns(t_ref.at[0])]
        store_registers(w1_ref, i, w1)
        product = suffix_product([1.0 - w for w in w1])
        ends = chunk_inflow(chunk_ladder(product[0]), none, one)
        gain = [d * ends for d in product]
        q_ref[pl.ds(lev, 1), :] = gain[0][0:1]

        @pl.when(lev == 0)
        def _():
            store_registers(gain_ref, 0, gain)

        w0 = [1.0 / (1.0 + c) for c in load_columns(t_ref.at[1])]
        store_registers(w0_ref, i, w0)
        r0 = [1.0 - w for w in w0]
        product = suffix_product(r0)
        steps = chunk_ladder(product[0])
        q_ref[pl.ds(lev + 4 * LEV, 1), :] = (product[0] * chunk_inflow(steps, none, one))[0:1]
        v = load_columns(t_ref.at[2])
        north = [jnp.maximum(x, 0.0) for x in v]
        south = [jnp.minimum(row_behind(x), 0.0) for x in v]
        store_registers(north0_ref, i, north)
        store_registers(south0_ref, i, south)
        rows = range(CHUNK)
        here = [w0[m] * (1.0 - north[m] + south[m]) * gain[m] for m in rows]
        upper = [w0[m] * north[m] * row_ahead(gain[m]) for m in rows]
        lower = [-w0[m] * south[m] * row_behind(gain[m]) for m in rows]
        for k, (ref, values) in enumerate(((here_ref, here), (upper_ref, upper), (lower_ref, lower))):
            store_registers(ref, i, values)
            first = suffix(values, r0)[0]
            total = first + product[0] * chunk_inflow(steps, first, none)
            q_ref[pl.ds(lev + (k + 1) * LEV, 1), :] = total[0:1]
        return carry

    lax.fori_loop(0, GROUP, level, 0)


def split(x):
    high = x.astype(BF16).astype(F32)
    return high, x - high


def product_nt(a, b):
    return lax.dot_general(a, b, (((1,), (1,)), ((), ())), preferred_element_type=F32)


def state_kernel(recv_ref, north_ref, up_ref, dn_ref, w1_hbm, w0_hbm, north0_hbm, south0_hbm, q1_ref,
                 send_ref, y_ref, flux_ref, rest_ref,
                 w1_ref, w0_ref, north0_ref, south0_ref, in_sems, x_ref, f1_ref, f0_ref, v_ref, hy_ref, q_ref, t_ref, term_ref, lhs_ref):
    is_top = top_flag()
    fetches = [
        pltpu.make_async_copy(source, target, in_sems.at[i])
        for i, (source, target) in enumerate(
            ((w1_hbm, w1_ref), (w0_hbm, w0_ref), (north0_hbm, north0_ref), (south0_hbm, south0_ref)))
    ]
    for fetch in fetches:
        fetch.start()
    for b in range(N_LAT):
        x_ref[:, b * 128:(b + 1) * 128] = recv_ref[b * 128:(b + 1) * 128, :].T

    def place(offset, n):
        cell = x_ref[offset + 36 + n:offset + 37 + n, :].astype(jnp.int32)
        return cell >> 7, cell & 127

    def make_terms(offset, n):
        parts = []
        for t in range(TR):
            value = x_ref[offset + 32 + 2 * n + t:offset + 33 + 2 * n + t, :]
            parts.append(split(value * x_ref[offset + n * LEV:offset + (n + 1) * LEV, :]))
        return parts

    group = 4
    for n in (1, 0):
        target = (f0_ref, f1_ref)[n]
        parts = make_terms(0, n)
        for t in range(TR):
            for p in range(2):
                term_ref[n, t, p] = parts[t][p]
        row, col = place(0, n)
        later = row >= HALF
        row = jnp.where(later, row - HALF, row)
        col = jnp.where(later, col + COLS, col)
        mask = jnp.where(iota((HALF, SLOTS), 0) == row, 1.0, 0.0).astype(BF16)
        hot = jnp.where(iota((2 * COLS, SLOTS), 0) == col, 1.0, 0.0).astype(BF16)
        for g in range(LEV // group):
            for i in range(group):
                for t in range(TR):
                    for p in range(2):
                        at = ((i * TR + t) * 2 + p) * HALF
                        term = term_ref[n, t, p, g * group + i:g * group + i + 1, :]
                        term = jnp.broadcast_to(term, (16, SLOTS)).astype(BF16)
                        lhs_ref[g % 2, at:at + HALF, :] = mask * jnp.concatenate([term] * 3, axis=0)
            out = product_nt(lhs_ref[g % 2], hot)
            for i in range(group):
                for t in range(TR):
                    at = (i * TR + t) * 2 * HALF
                    both = out[at:at + HALF] + out[at + HALF:at + 2 * HALF]
                    target[t * LEV + g * group + i, TOP:TOP + HALF, :] = both[:, :COLS]
                    target[t * LEV + g * group + i, TOP + HALF:END, :] = both[:, COLS:]

    edges = {}
    for side, offset in ((0, FIELDS), (1, 2 * FIELDS)):
        for n in (1, 0):
            rows = ((ROWS - 1, ROWS - 2), (0, 1))[side][:2 if n else 1]
            row, col = place(offset, n)
            hot = jnp.where(iota((COLS, SLOTS), 0) == col, 1.0, 0.0).astype(BF16)
            parts = make_terms(offset, n)
            stack = []
            for r in rows:
                hit = jnp.where(row == r, 1.0, 0.0)
                for t in range(TR):
                    for p in range(2):
                        stack.append((parts[t][p] * hit).astype(BF16))
            out = product_nt(jnp.concatenate(stack, axis=0), hot)
            for i in range(len(rows)):
                for t in range(TR):
                    at = (i * TR + t) * 2 * LEV
                    edges[side, n, i, t] = out[at:at + LEV] + out[at + LEV:at + 2 * LEV]

    hy_ref[...] = jnp.zeros(hy_ref.shape, F32)
    for side in range(2):
        for t in range(TR):
            near = edges[side, 1, 0, t]
            far = edges[side, 1, 1, t]
            inner = f1_ref[t * LEV:(t + 1) * LEV, TOP if side == 0 else END - 1, :]
            if side == 0:
                north = jnp.maximum(up_ref[2], 0.0)
                south = jnp.minimum(up_ref[1], 0.0)
                y = near + north * (inner - near) + south * (near - far)
            else:
                north = jnp.maximum(dn_ref[0], 0.0)
                south = jnp.minimum(jnp.where(is_top, 0.0, north_ref[1, :, ROWS - 1, :]), 0.0)
                y = near + north * (far - near) + south * (near - inner)
            at = TOP - 1 if side == 0 else END
            slot = 31 if side == 0 else 0
            edge0 = edges[side, 0, 0, t]
            for lev in range(LEV):
                hy_ref[t * LEV + lev, slot:slot + 1, :] = y[lev:lev + 1, :]
                f1_ref[t * LEV + lev, at:at + 1, :] = near[lev:lev + 1, :]
                f0_ref[t * LEV + lev, at:at + 1, :] = edge0[lev:lev + 1, :]
    for lev in range(LEV):
        v_ref[1, lev, TOP - 1:TOP, :] = up_ref[2, lev:lev + 1, :]
        v_ref[0, lev, TOP - 1:TOP, :] = up_ref[0, lev:lev + 1, :]
    for t in range(TR):
        flux_ref[t] = f1_ref[t * LEV, TOP:END, :] + f0_ref[t * LEV, TOP:END, :]

    for fetch in fetches:
        fetch.wait()

    def level(lev, carry):
        none = jnp.zeros((8, 128), F32)
        north = [None, None]
        south = [None, None]
        for n in range(STEPS):
            v = masked_north(north_ref[n, lev], is_top)
            v_ref[n, lev, TOP:END, :] = v
            north[n] = jnp.maximum(v, 0.0)
            south[n] = jnp.minimum(v_ref[n, lev, TOP - 1:END - 1, :], 0.0)
        for t in range(TR):
            at = t * LEV + lev
            for n, ref in ((1, f1_ref), (0, f0_ref)):
                a = ref[at, TOP:END, :]
                y = a + north[n] * (ref[at, TOP + 1:END + 1, :] - a) + south[n] * (a - ref[at, TOP - 1:END - 1, :])
                edge = hy_ref[at] if n else jnp.zeros((32, COLS), F32)
                t_ref[2 * t + n] = jnp.concatenate([y, edge], axis=0).T
        w1 = load_registers(w1_ref, lev)
        r1 = [1.0 - w for w in w1]
        product1 = suffix_product(r1)
        steps1 = chunk_ladder(product1[0])
        w0 = load_registers(w0_ref, lev)
        r0 = [1.0 - w for w in w0]
        product0 = suffix_product(r0)[0]
        steps0 = chunk_ladder(product0)
        for t in range(TR):
            at = t * LEV + lev
            y = load_columns(t_ref.at[2 * t + 1])
            part = suffix([w1[m] * y[m] for m in range(CHUNK)], r1)
            inflow = chunk_inflow(steps1, part[0], none)
            rest = [part[m] + product1[m] * inflow for m in range(CHUNK)]
            q_ref[pl.ds(at, 1), :] = rest[0][0:1]

            @pl.when(lev == 0)
            def _():
                store_registers(rest_ref, t, rest)

            y = load_columns(t_ref.at[2 * t])
            north0 = load_registers(north0_ref, lev)
            south0 = load_registers(south0_ref, lev)
            total = [
                w0[m] * (y[m] + rest[m] + north0[m] * (row_ahead(rest[m]) - rest[m])
                         + south0[m] * (rest[m] - row_behind(rest[m])))
                for m in range(CHUNK)
            ]
            store_registers(y_ref, at, total)
            first = suffix(total, r0)[0]
            first = first + product0 * chunk_inflow(steps0, first, none)
            q_ref[pl.ds(TR * LEV + at, 1), :] = first[0:1]
        return carry

    lax.fori_loop(0, LEV, level, 0)
    q2 = q_ref[...]
    q1 = q1_ref[...]
    for j in range(N_LON):
        send_ref[j, 0:REST, :] = q2
        send_ref[j, REST:, :] = q1


def final_kernel(recv_ref, y_ref, here_ref, upper_ref, lower_ref, w0_ref, gain_ref, rest_ref, f_ref,
                 adj_ref, flux_ref, in1_ref, in0_ref, flow_ref, t_ref):
    me = lax.axis_index("lon")

    def part(j, i):
        return recv_ref[j, i * LEV:(i + 1) * LEV, :]

    for t in range(TR):
        lo, hi = t * LEV, (t + 1) * LEV
        gain = jnp.ones((LEV, 128), F32)
        rest = jnp.zeros((LEV, 128), F32)
        for j in range(N_LON - 1, -1, -1):
            g = part(j, 4)
            rest = g * rest + part(j, t)
            gain = g * gain
        inflow = rest / (1.0 - gain)
        gain = jnp.ones((LEV, 128), F32)
        rest = jnp.zeros((LEV, 128), F32)
        for j in range(N_LON - 1, -1, -1):
            in1_ref[j, lo:hi, :] = inflow
            total = part(j, TR + t) + part(j, 5) * inflow
            total = total + part(j, 6) * row_ahead(inflow) + part(j, 7) * row_behind(inflow)
            in0_ref[j, lo:hi, :] = total
            inflow = part(j, 4) * inflow + part(j, t)
            g = part(j, 8)
            rest = g * rest + total
            gain = g * gain
        inflow = rest / (1.0 - gain)
        for j in range(N_LON - 1, -1, -1):
            total = in0_ref[j, lo:hi, :]
            in0_ref[j, lo:hi, :] = inflow
            inflow = part(j, 8) * inflow + total
        mine = in1_ref[me, lo:hi, :]
        flow_ref[0, lo:hi, :] = mine
        flow_ref[1, lo:hi, :] = row_ahead(mine)
        flow_ref[2, lo:hi, :] = row_behind(mine)
        flow_ref[3, lo:hi, :] = in0_ref[me, lo:hi, :]

    def back(values, slot):
        for m in range(CHUNK):
            t_ref[slot, pl.ds(m, 8, stride=CHUNK), :] = values[m]
        return t_ref[slot].T[0:ROWS]

    for t in range(TR):
        flow = flow_ref[0, t * LEV:t * LEV + 1, :]
        rest = load_registers(rest_ref, t)
        gain = load_registers(gain_ref, 0)
        flux_ref[t] = f_ref[t] + back([rest[m] + gain[m] * flow for m in range(CHUNK)], t)

    def level(lev, carry):
        w0 = load_registers(w0_ref, lev)
        r0 = [1.0 - w for w in w0]
        product = suffix_product(r0)
        steps = chunk_ladder(product[0])
        here = load_registers(here_ref, lev)
        upper = load_registers(upper_ref, lev)
        lower = load_registers(lower_ref, lev)
        for t in range(TR):
            at = t * LEV + lev
            y = load_registers(y_ref, at)
            flow, ahead, behind, inflow = (flow_ref[i, pl.ds(at, 1), :] for i in range(4))
            total = [y[m] + here[m] * flow + upper[m] * ahead + lower[m] * behind for m in range(CHUNK)]
            value = suffix(total, r0)
            enter = chunk_inflow(steps, value[0], inflow)
            adj_ref[t, lev] = back([value[m] + product[m] * enter for m in range(CHUNK)], t)
        return carry

    lax.fori_loop(0, LEV, level, 0)


def whole(shape):
    return pl.BlockSpec(shape, lambda i: (0,) * len(shape))


def in_hbm(*arrays):
    return [pltpu.with_memory_space_constraint(x, pltpu.HBM) for x in arrays]


ANYWHERE = pl.BlockSpec(memory_space=pltpu.HBM)


def call(kernel, steps, outs, in_specs, scratch, name, mega, cost=None):
    return pl.pallas_call(
        kernel,
        grid=(steps,),
        out_shape=[pltpu.HBM(s, F32) if hbm else jax.ShapeDtypeStruct(s, F32) for s, _, hbm in outs],
        in_specs=in_specs,
        out_specs=[whole(s) if spec is None else spec for s, spec, _ in outs],
        scratch_shapes=[pltpu.VMEM(*s) if isinstance(s, tuple) else s for s in scratch],
        compiler_params=pltpu.CompilerParams(vmem_limit_bytes=mega * MEGA),
        cost_estimate=cost,
        name=name,
    )


def shards(east, north, kernels, departures, cells, counts):
    send, up, dn = call(
        pack_kernel, 1,
        [((SLOTS, 128), None, True), ((4, LEV, COLS), None, False), ((2, LEV, COLS), None, False)],
        [ANYWHERE] * 6,
        [(kernels.shape, F32), (departures.shape, F32), (cells.shape, jnp.int32), (counts.shape, jnp.int32),
         ((STEPS, LEV, 8, COLS), F32), ((LEV, 8, COLS), F32), ((LEV, 8, COLS), F32), ((LEV, 8, COLS), F32),
         ((FIELDS, SLOTS), F32), pltpu.SemaphoreType.DMA((8,))],
        "pack", 8,
    )(*in_hbm(kernels, departures, cells, counts, north, east))
    recv = lax.all_to_all(send.reshape(128, 8, 128), ("lat", "lon"), split_axis=0, concat_axis=0, tiled=True)
    up = lax.ppermute(up, "lat", [(i, i + 1) for i in range(N_LAT - 1)])
    dn = lax.ppermute(dn, "lat", [(i + 1, i) for i in range(N_LAT - 1)])
    turned = (LEV, 128, 128)
    some = pl.BlockSpec((GROUP, 128, 128), lambda i: (i, 0, 0))
    w1, w0, north0, south0, here, upper, lower, gain, q1 = call(
        coef_kernel, LEV // GROUP,
        [(turned, some, True)] * 7 + [((1, 128, 128), None, True), ((COEF, 128), None, False)],
        [whole(east.shape), pl.BlockSpec((1, LEV, ROWS, COLS), lambda i: (0, 0, 0, 0)), whole(up.shape), whole(dn.shape)],
        [((LEV, 32, COLS), F32), ((LEV, 32, COLS), F32), ((3, 128, 128), F32)],
        "coef", 16, pl.CostEstimate(flops=2 * 10**8, transcendentals=0, bytes_accessed=6 * 10**7),
    )(east, north, up, dn)
    tiles = (TR * LEV, 128, 128)
    send2, y, f, rest = call(
        state_kernel, 1,
        [((N_LON, REST + COEF, 128), None, False), (tiles, None, False), ((TR, ROWS, COLS), None, False),
         ((TR, 128, 128), None, False)],
        [whole((SLOTS, 128)), whole(north.shape), whole(up.shape), whole(dn.shape)] + [ANYWHERE] * 4 + [whole(q1.shape)],
        [(turned, F32)] * 4 + [pltpu.SemaphoreType.DMA((4,)),
         ((128, SLOTS), F32), ((TR * LEV, PAD, COLS), F32), ((TR * LEV, PAD, COLS), F32),
         ((STEPS, LEV, PAD, COLS), F32), ((TR * LEV, 32, COLS), F32), ((REST, 128), F32), ((4, 128, 128), F32),
         ((STEPS, TR, 2, LEV, SLOTS), F32), ((2, 16 * HALF, SLOTS), BF16)],
        "state", 32,
    )(recv.reshape(SLOTS, 128), north, up, dn, *in_hbm(w1, w0, north0, south0), q1)
    recv2 = lax.all_to_all(send2, "lon", split_axis=0, concat_axis=0, tiled=True)
    adjoint, flux = call(
        final_kernel, 1,
        [((TR, LEV, ROWS, COLS), None, True), ((TR, ROWS, COLS), None, True)],
        [whole(recv2.shape), whole(tiles)] + [whole(turned)] * 4 + [whole(gain.shape), whole(rest.shape), whole(f.shape)],
        [((N_LON, TR * LEV, 128), F32), ((N_LON, TR * LEV, 128), F32), ((4, TR * LEV, 128), F32),
         ((2, 128, 128), F32)],
        "final", 24,
    )(recv2, y, here, upper, lower, w0, gain, rest, f)
    return adjoint, flux


def solution(mesh):
    return jax.shard_map(
        shards,
        mesh=mesh,
        in_specs=(
            P(None, None, "lat", "lon"),
            P(None, None, "lat", "lon"),
            P(None, None, ("lat", "lon")),
            P(None, None, ("lat", "lon")),
            P(None, ("lat", "lon")),
            P(None, ("lat", "lon")),
        ),
        out_specs=(P(None, None, "lat", "lon"), P(None, "lat", "lon")),
        check_vma=False,
    )
```

```python
import jax
import jax.numpy as jnp
from jax import lax
from jax.experimental import pallas as pl
from jax.experimental.pallas import tpu as pltpu
from jax.sharding import PartitionSpec as P

F32 = jnp.float32
BF16 = jnp.bfloat16
STEPS, TR, LEV, ROWS, COLS = 2, 2, 16, 96, 128
SLOTS = 1024
N_LAT, N_LON = 8, 16
PAD = 112
TOP = 8
END = TOP + ROWS
HALF = ROWS // 2
FIELDS = 40
COEF = 5 * LEV
REST = 4 * LEV
PAYLOAD = 8 * LEV
GROUP = 4
ABREAST = 8
FINAL_ABREAST = 8
CHUNK = 16
MEGA = 1024 * 1024


def iota(shape, dim):
    return lax.broadcasted_iota(jnp.int32, shape, dim)


def row_ahead(x):
    return pltpu.roll(x, 127, 1)


def row_behind(x):
    return pltpu.roll(x, 1, 1)


def chunk_ahead(x, k):
    return pltpu.roll(x, 8 - k, 0)


def load_columns(ref):
    return [ref[pl.ds(m, 8, stride=CHUNK), :] for m in range(CHUNK)]


def load_registers(ref, lead):
    return [ref[lead, 8 * m:8 * m + 8, :] for m in range(CHUNK)]


def store_registers(ref, lead, values):
    for m in range(CHUNK):
        ref[lead, 8 * m:8 * m + 8, :] = values[m]


def suffix(values, retain):
    out = [None] * CHUNK
    out[-1] = values[-1]
    for m in range(CHUNK - 2, -1, -1):
        out[m] = values[m] + retain[m] * out[m + 1]
    return out


def suffix_product(retain):
    out = [None] * CHUNK
    out[-1] = retain[-1]
    for m in range(CHUNK - 2, -1, -1):
        out[m] = retain[m] * out[m + 1]
    return out


def chunk_ladder(product):
    last = iota(product.shape, 0) == 7
    steps = []
    value = jnp.where(last, 0.0, chunk_ahead(product, 1))
    for k in (1, 2, 4):
        steps.append((k, value))
        if k < 4:
            value = value * chunk_ahead(value, k)
    return steps


def chunk_inflow(steps, first, inflow):
    value = jnp.where(iota(first.shape, 0) == 7, inflow, chunk_ahead(first, 1))
    for k, product in steps:
        value = value + product * chunk_ahead(value, k)
    return value


def masked_north(v, is_top):
    return jnp.where((iota(v.shape, 0) == ROWS - 1) & is_top, 0.0, v)


def top_flag():
    return lax.axis_index("lat") == N_LAT - 1


def pack_kernel(ker_hbm, dep_hbm, cell_hbm, cnt_hbm, north_hbm, east_hbm,
                send_hbm, up_ref, dn_ref,
                ker_ref, dep_ref, cell_ref, cnt_ref, nlast_ref, nfirst_ref, elast_ref, efirst_ref, x_ref, send_ref, sems, out_sems):
    copies = [
        pltpu.make_async_copy(cnt_hbm, cnt_ref, sems.at[0]),
        pltpu.make_async_copy(dep_hbm, dep_ref, sems.at[1]),
        pltpu.make_async_copy(cell_hbm, cell_ref, sems.at[2]),
        pltpu.make_async_copy(ker_hbm, ker_ref, sems.at[3]),
        pltpu.make_async_copy(north_hbm.at[:, :, ROWS - 8:, :], nlast_ref, sems.at[4]),
        pltpu.make_async_copy(north_hbm.at[1, :, :8, :], nfirst_ref, sems.at[5]),
        pltpu.make_async_copy(east_hbm.at[1, :, ROWS - 8:, :], elast_ref, sems.at[6]),
        pltpu.make_async_copy(east_hbm.at[1, :, :8, :], efirst_ref, sems.at[7]),
    ]
    for copy in copies:
        copy.start()
    spread = jnp.where(iota((128, SLOTS), 1) // 8 == iota((128, SLOTS), 0), 1.0, 0.0).astype(BF16)
    within = (iota((8, SLOTS), 1) % 8).astype(F32)
    for copy in copies[:4]:
        copy.wait()
    for n in range(STEPS):
        x_ref[n * LEV:(n + 1) * LEV, :] = ker_ref[n]
    counts = jnp.concatenate([cnt_ref[...].astype(F32), jnp.zeros((6, 128), F32)], axis=0)
    counts = jnp.dot(counts.astype(BF16), spread, preferred_element_type=F32)
    live = jnp.where(within < counts, 1.0, 0.0)
    rows = []
    for n in range(STEPS):
        rows.append(dep_ref[n] * live[n:n + 1])
    rows.append(cell_ref[...].astype(F32))
    rows.append(jnp.zeros((2, SLOTS), F32))
    x_ref[2 * LEV:FIELDS, :] = jnp.concatenate(rows, axis=0)
    none = jnp.zeros((FIELDS, 128), F32)

    def lanes(b):
        if b < 0 or b >= N_LAT:
            return none
        return x_ref[:, b * 128:(b + 1) * 128]

    outs = []
    for b in range(N_LAT):
        tile = jnp.concatenate([lanes(b), lanes(b - 1), lanes(b + 1), jnp.zeros((8, 128), F32)], axis=0)
        block = pl.ds(b * 128, 128)
        send_ref[b * 128:(b + 1) * 128, :] = tile.T
        outs.append(pltpu.make_async_copy(send_ref.at[block], send_hbm.at[block], out_sems.at[b]))
        outs[-1].start()
    for copy in copies[4:]:
        copy.wait()
    up_ref[0] = nlast_ref[0, :, 7, :]
    up_ref[1] = nlast_ref[1, :, 6, :]
    up_ref[2] = nlast_ref[1, :, 7, :]
    up_ref[3] = elast_ref[:, 7, :]
    dn_ref[0] = nfirst_ref[:, 0, :]
    dn_ref[1] = efirst_ref[:, 0, :]
    for copy in outs:
        copy.wait()


def coef_kernel(east_ref, north_ref, up_ref, dn_ref,
                w1_hbm, w0_hbm, v0_hbm, here_hbm, upper_hbm, lower_hbm, gain_ref, q_ref,
                w1_ref, w0_ref, v0_ref, here_ref, upper_ref, lower_ref, sems,
                he_ref, hv_ref, t_ref):
    is_top = top_flag()
    he_ref[...] = jnp.zeros(he_ref.shape, F32)
    hv_ref[...] = jnp.zeros(hv_ref.shape, F32)
    for lev in range(LEV):
        he_ref[lev, 0:1, :] = dn_ref[1, lev:lev + 1, :]
        he_ref[lev, 31:32, :] = up_ref[3, lev:lev + 1, :]
        hv_ref[lev, 31:32, :] = up_ref[0, lev:lev + 1, :]
    outs = ((w1_ref, w1_hbm), (w0_ref, w0_hbm), (v0_ref, v0_hbm), (here_ref, here_hbm), (upper_ref, upper_hbm),
            (lower_ref, lower_hbm))

    def level(lev, slot):
        t_ref[slot, 0] = jnp.concatenate([east_ref[1, lev], he_ref[lev]], axis=0).T
        t_ref[slot, 1] = jnp.concatenate([east_ref[0, lev], jnp.zeros((32, COLS), F32)], axis=0).T
        t_ref[slot, 2] = jnp.concatenate([masked_north(north_ref[0, lev], is_top), hv_ref[lev]], axis=0).T
        one = jnp.ones((8, 128), F32)
        none = jnp.zeros((8, 128), F32)
        w1 = [1.0 / (1.0 + c) for c in load_columns(t_ref.at[slot, 0])]
        store_registers(w1_ref, lev, w1)
        product = suffix_product([1.0 - w for w in w1])
        ends = chunk_inflow(chunk_ladder(product[0]), none, one)
        gain = [d * ends for d in product]
        q_ref[lev:lev + 1, :] = gain[0][0:1]

        if lev == 0:
            store_registers(gain_ref, 0, gain)


        w0 = [1.0 / (1.0 + c) for c in load_columns(t_ref.at[slot, 1])]
        store_registers(w0_ref, lev, w0)
        r0 = [1.0 - w for w in w0]
        product = suffix_product(r0)
        steps = chunk_ladder(product[0])
        q_ref[lev + 4 * LEV:lev + 4 * LEV + 1, :] = (product[0] * chunk_inflow(steps, none, one))[0:1]
        v = load_columns(t_ref.at[slot, 2])
        store_registers(v0_ref, lev, v)
        rows = range(CHUNK)
        north = [jnp.maximum(x, 0.0) for x in v]
        south = [jnp.minimum(x, 0.0) for x in v]
        beyond = [row_ahead(x) for x in gain]
        here = [w0[m] * ((1.0 - north[m]) * gain[m] + row_behind(south[m] * beyond[m])) for m in rows]
        upper = [w0[m] * north[m] * beyond[m] for m in rows]
        lower = [-w0[m] * row_behind(south[m] * gain[m]) for m in rows]
        for k, (ref, values) in enumerate(((here_ref, here), (upper_ref, upper), (lower_ref, lower))):
            store_registers(ref, lev, values)
            first = suffix(values, r0)[0]
            total = first + product[0] * chunk_inflow(steps, first, none)
            q_ref[lev + (k + 1) * LEV:lev + (k + 1) * LEV + 1, :] = total[0:1]

    copies = []
    for g in range(LEV // GROUP):
        for lev in range(g * GROUP, (g + 1) * GROUP):
            level(lev, lev % ABREAST)
        for i, (source, target) in enumerate(outs):
            part = pl.ds(g * GROUP, GROUP)
            copies.append(pltpu.make_async_copy(source.at[part], target.at[part], sems.at[g, i]))
            copies[-1].start()
    for copy in copies:
        copy.wait()


def split(x):
    high = x.astype(BF16).astype(F32)
    return high, x - high


def product_nt(a, b):
    return lax.dot_general(a, b, (((1,), (1,)), ((), ())), preferred_element_type=F32)


def state_kernel(recv_ref, north_ref, up_ref, dn_ref, w1_hbm, w0_hbm, v0_hbm, q1_ref,
                 send_ref, y_ref, flux_ref, rest_ref,
                 w1_ref, w0_ref, v0_ref, in_sems, x_ref, f1_ref, f0_ref, v_ref, e_ref, q_ref, t_ref, term_ref, lhs_ref, mask_ref, hot_ref):
    is_top = top_flag()
    fetches = [
        pltpu.make_async_copy(source, target, in_sems.at[i])
        for i, (source, target) in enumerate(
            ((w1_hbm, w1_ref), (w0_hbm, w0_ref), (v0_hbm, v0_ref)))
    ]
    for fetch in fetches:
        fetch.start()
    for b in range(N_LAT):
        x_ref[:, b * 128:(b + 1) * 128] = recv_ref[b * 128:(b + 1) * 128, :].T

    def place(offset, n):
        cell = x_ref[offset + 36 + n:offset + 37 + n, :].astype(jnp.int32)
        return cell >> 7, cell & 127

    def make_terms(offset, n):
        parts = []
        for t in range(TR):
            value = x_ref[offset + 32 + 2 * n + t:offset + 33 + 2 * n + t, :]
            parts.append(split(value * x_ref[offset + n * LEV:offset + (n + 1) * LEV, :]))
        return parts

    for n in (1, 0):
        parts = make_terms(0, n)
        for t in range(TR):
            for p in range(2):
                term_ref[n, t, p] = parts[t][p]
        row, _ = place(0, n)
        later = row >= HALF
        row = jnp.where(later, row - HALF, row)
        mask_ref[n] = jnp.where(iota((HALF, SLOTS), 0) == row, 1.0, 0.0).astype(BF16)
        cell = recv_ref[:, 36 + n:37 + n].astype(jnp.int32)
        col = (cell & 127) + jnp.where(cell >= HALF * COLS, COLS, 0)
        hot_ref[n] = jnp.where(iota((SLOTS, 2 * COLS), 1) == col, 1.0, 0.0).astype(BF16)

    def deposit(g):
        for n in (1, 0):
            target = (f0_ref, f1_ref)[n]
            for i in range(GROUP):
                for t in range(TR):
                    for p in range(2):
                        at = ((i * TR + t) * 2 + p) * HALF
                        term = term_ref[n, t, p, g * GROUP + i:g * GROUP + i + 1, :]
                        term = jnp.broadcast_to(term, (16, SLOTS)).astype(BF16)
                        lhs_ref[n, at:at + HALF, :] = mask_ref[n] * jnp.concatenate([term] * 3, axis=0)
            out = jnp.dot(lhs_ref[n], hot_ref[n], preferred_element_type=F32)
            for i in range(GROUP):
                for t in range(TR):
                    at = (i * TR + t) * 2 * HALF
                    both = out[at:at + HALF] + out[at + HALF:at + 2 * HALF]
                    target[t * LEV + g * GROUP + i, TOP:TOP + HALF, :] = both[:, :COLS]
                    target[t * LEV + g * GROUP + i, TOP + HALF:END, :] = both[:, COLS:]

    edges = {}
    for side, offset in ((0, FIELDS), (1, 2 * FIELDS)):
        for n in (1, 0):
            rows = ((ROWS - 1, ROWS - 2), (0, 1))[side][:2 if n else 1]
            row, col = place(offset, n)
            hot = jnp.where(iota((COLS, SLOTS), 0) == col, 1.0, 0.0).astype(BF16)
            parts = make_terms(offset, n)
            stack = []
            for r in rows:
                hit = jnp.where(row == r, 1.0, 0.0)
                for t in range(TR):
                    for p in range(2):
                        stack.append((parts[t][p] * hit).astype(BF16))
            out = product_nt(jnp.concatenate(stack, axis=0), hot)
            for i in range(len(rows)):
                for t in range(TR):
                    at = (i * TR + t) * 2 * LEV
                    edges[side, n, i, t] = out[at:at + LEV] + out[at + LEV:at + 2 * LEV]

    for (side, n, i, t), value in edges.items():
        if n == 1:
            e_ref[side, i, t] = value
        at = TOP - 1 if side == 0 else END
        if i == 0:
            for lev in range(LEV):
                (f0_ref, f1_ref)[n][t * LEV + lev, at:at + 1, :] = value[lev:lev + 1, :]
    for lev in range(LEV):
        v_ref[1, lev, TOP - 1:TOP, :] = up_ref[2, lev:lev + 1, :]
        v_ref[0, lev, TOP - 1:TOP, :] = up_ref[0, lev:lev + 1, :]
    low_north = jnp.maximum(up_ref[2], 0.0)
    low_south = jnp.minimum(up_ref[1], 0.0)
    high_north = jnp.maximum(dn_ref[0], 0.0)
    high_south = jnp.minimum(jnp.where(is_top, 0.0, north_ref[1, :, ROWS - 1, :]), 0.0)
    deposit(0)
    for fetch in fetches:
        fetch.wait()

    def edge_rows(lev, t):
        at = t * LEV + lev
        one = slice(lev, lev + 1)
        low, below = e_ref[0, 0, t, one, :], e_ref[0, 1, t, one, :]
        low = low + low_north[one] * (f1_ref[at, TOP:TOP + 1, :] - low) + low_south[one] * (low - below)
        high, above = e_ref[1, 0, t, one, :], e_ref[1, 1, t, one, :]
        high = high + high_north[one] * (above - high) + high_south[one] * (high - f1_ref[at, END - 1:END, :])
        row = iota((32, COLS), 0)
        return jnp.where(row == 0, high, jnp.where(row == 31, low, 0.0))

    def level(lev):
        none = jnp.zeros((8, 128), F32)
        north = [None, None]
        south = [None, None]
        for n in range(STEPS):
            v = masked_north(north_ref[n, lev], is_top)
            v_ref[n, lev, TOP:END, :] = v
            north[n] = jnp.maximum(v, 0.0)
            south[n] = jnp.minimum(v_ref[n, lev, TOP - 1:END - 1, :], 0.0)
        for t in range(TR):
            at = t * LEV + lev
            for n, ref in ((1, f1_ref), (0, f0_ref)):
                a = ref[at, TOP:END, :]
                y = a + north[n] * (ref[at, TOP + 1:END + 1, :] - a) + south[n] * (a - ref[at, TOP - 1:END - 1, :])
                edge = edge_rows(lev, t) if n else jnp.zeros((32, COLS), F32)
                t_ref[2 * t + n] = jnp.concatenate([y, edge], axis=0).T
        w1 = load_registers(w1_ref, lev)
        r1 = [1.0 - w for w in w1]
        product1 = suffix_product(r1)
        steps1 = chunk_ladder(product1[0])
        w0 = load_registers(w0_ref, lev)
        r0 = [1.0 - w for w in w0]
        product0 = suffix_product(r0)[0]
        steps0 = chunk_ladder(product0)
        for t in range(TR):
            at = t * LEV + lev
            y = load_columns(t_ref.at[2 * t + 1])
            part = suffix([w1[m] * y[m] for m in range(CHUNK)], r1)
            inflow = chunk_inflow(steps1, part[0], none)
            rest = [part[m] + product1[m] * inflow for m in range(CHUNK)]
            q_ref[at:at + 1, :] = rest[0][0:1]

            if lev == 0:
                store_registers(rest_ref, t, rest)

            y = load_columns(t_ref.at[2 * t])
            v0 = load_registers(v0_ref, lev)
            rise = [row_ahead(x) - x for x in rest]
            total = [
                w0[m] * (y[m] + rest[m] + jnp.maximum(v0[m], 0.0) * rise[m]
                         + row_behind(jnp.minimum(v0[m], 0.0) * rise[m]))
                for m in range(CHUNK)
            ]
            store_registers(y_ref, at, total)
            first = suffix(total, r0)[0]
            first = first + product0 * chunk_inflow(steps0, first, none)
            q_ref[TR * LEV + at:TR * LEV + at + 1, :] = first[0:1]

    for g in range(LEV // GROUP):
        if g + 1 < LEV // GROUP:
            deposit(g + 1)
        for lev in range(g * GROUP, (g + 1) * GROUP):
            level(lev)
    for t in range(TR):
        flux_ref[t] = f1_ref[t * LEV, TOP:END, :] + f0_ref[t * LEV, TOP:END, :]
    q1 = q1_ref[...]
    gamma = q1[3 * LEV:4 * LEV]
    spare = iota((LEV, 128), 1) >= ROWS
    rows = [q_ref[0:TR * LEV, :]]
    for i, base in enumerate((q_ref[TR * LEV:TR * LEV + LEV, :], q_ref[TR * LEV + LEV:, :], q1[LEV:2 * LEV])):
        rows.append(jnp.where(spare, pltpu.roll(gamma, ROWS - 32 * i, 1), base))
    rows += [q1[0:LEV], q1[2 * LEV:3 * LEV], q1[4 * LEV:]]
    payload = jnp.concatenate(rows, axis=0)
    for j in range(N_LON):
        send_ref[j] = payload


def final_kernel(recv_ref, y_ref, here_ref, upper_ref, lower_ref, w0_ref, gain_ref, rest_ref, f_ref,
                 adj_hbm, flux_ref, adj_ref, sems, gamma_ref, in1_ref, in0_ref, flow_ref, t_ref):
    me = lax.axis_index("lon")

    def part(j, i):
        return recv_ref[j, i * LEV:(i + 1) * LEV, :]

    lane = iota((LEV, 128), 1)

    def gamma(j):
        first, second, third = (pltpu.roll(part(j, 2 + i), 32 * (i + 1), 1) for i in range(3))
        return jnp.where(lane < 32, first, jnp.where(lane < 64, second, third))

    for j in range(N_LON):
        gamma_ref[j] = gamma(j)

    def both(x):
        return jnp.concatenate([x, x], axis=0)

    pair = (TR * LEV, 128)
    gain = jnp.ones((LEV, 128), F32)
    rest = jnp.zeros(pair, F32)
    for j in range(N_LON - 1, -1, -1):
        g = part(j, 5)
        rest = both(g) * rest + recv_ref[j, 0:TR * LEV, :]
        gain = g * gain
    inflow = rest * both(1.0 / (1.0 - gain))
    gain = jnp.ones((LEV, 128), F32)
    rest = jnp.zeros(pair, F32)
    for j in range(N_LON - 1, -1, -1):
        in1_ref[j] = inflow
        total = recv_ref[j, TR * LEV:2 * TR * LEV, :] + both(part(j, 4)) * inflow
        total = total + both(part(j, 6)) * row_ahead(inflow) + both(gamma_ref[j]) * row_behind(inflow)
        in0_ref[j] = total
        inflow = both(part(j, 5)) * inflow + recv_ref[j, 0:TR * LEV, :]
        g = part(j, 7)
        rest = both(g) * rest + total
        gain = g * gain
    inflow = rest * both(1.0 / (1.0 - gain))
    for j in range(N_LON - 1, -1, -1):
        total = in0_ref[j]
        in0_ref[j] = inflow
        inflow = both(part(j, 7)) * inflow + total
    mine = in1_ref[me]
    flow_ref[0] = mine
    flow_ref[1] = row_ahead(mine)
    flow_ref[2] = row_behind(mine)
    flow_ref[3] = in0_ref[me]

    def back(values, slot):
        for m in range(CHUNK):
            t_ref[slot, pl.ds(m, 8, stride=CHUNK), :] = values[m]
        return t_ref[slot].T[0:ROWS]

    for t in range(TR):
        flow = flow_ref[0, t * LEV:t * LEV + 1, :]
        rest = load_registers(rest_ref, t)
        gain = load_registers(gain_ref, 0)
        flux_ref[t] = f_ref[t] + back([rest[m] + gain[m] * flow for m in range(CHUNK)], t)

    def level(lev, base):
        w0 = load_registers(w0_ref, lev)
        r0 = [1.0 - w for w in w0]
        product = suffix_product(r0)
        steps = chunk_ladder(product[0])
        here = load_registers(here_ref, lev)
        upper = load_registers(upper_ref, lev)
        lower = load_registers(lower_ref, lev)
        for t in range(TR):
            at = t * LEV + lev
            y = load_registers(y_ref, at)
            flow, ahead, behind, inflow = (flow_ref[i, at:at + 1, :] for i in range(4))
            total = [y[m] + here[m] * flow + upper[m] * ahead + lower[m] * behind for m in range(CHUNK)]
            value = suffix(total, r0)
            enter = chunk_inflow(steps, value[0], inflow)
            adj_ref[t, lev] = back([value[m] + product[m] * enter for m in range(CHUNK)], base + t)

    copies = []
    for g in range(LEV // GROUP):
        for lev in range(g * GROUP, (g + 1) * GROUP):
            level(lev, TR * (lev % FINAL_ABREAST))
        for t in range(TR):
            part_of = pl.ds(g * GROUP, GROUP)
            copies.append(pltpu.make_async_copy(adj_ref.at[t, part_of], adj_hbm.at[t, part_of], sems.at[g, t]))
            copies[-1].start()
    for copy in copies:
        copy.wait()


def whole(shape):
    return pl.BlockSpec(shape, lambda i: (0,) * len(shape))


def in_hbm(*arrays):
    return [pltpu.with_memory_space_constraint(x, pltpu.HBM) for x in arrays]


ANYWHERE = pl.BlockSpec(memory_space=pltpu.HBM)


def call(kernel, steps, outs, in_specs, scratch, name, mega, cost=None):
    return pl.pallas_call(
        kernel,
        grid=(steps,),
        out_shape=[pltpu.HBM(s, F32) if hbm else jax.ShapeDtypeStruct(s, F32) for s, _, hbm in outs],
        in_specs=in_specs,
        out_specs=[whole(s) if spec is None else spec for s, spec, _ in outs],
        scratch_shapes=[pltpu.VMEM(*s) if isinstance(s, tuple) else s for s in scratch],
        compiler_params=pltpu.CompilerParams(vmem_limit_bytes=mega * MEGA),
        cost_estimate=cost,
        name=name,
    )


def shards(east, north, kernels, departures, cells, counts):
    send, up, dn = call(
        pack_kernel, 1,
        [((SLOTS, 128), ANYWHERE, True), ((4, LEV, COLS), None, False), ((2, LEV, COLS), None, False)],
        [ANYWHERE] * 6,
        [(kernels.shape, F32), (departures.shape, F32), (cells.shape, jnp.int32), (counts.shape, jnp.int32),
         ((STEPS, LEV, 8, COLS), F32), ((LEV, 8, COLS), F32), ((LEV, 8, COLS), F32), ((LEV, 8, COLS), F32),
         ((FIELDS, SLOTS), F32), ((SLOTS, 128), F32), pltpu.SemaphoreType.DMA((8,)),
         pltpu.SemaphoreType.DMA((N_LAT,))],
        "pack", 8,
    )(*in_hbm(kernels, departures, cells, counts, north, east))
    recv = lax.all_to_all(send.reshape(128, 8, 128), ("lat", "lon"), split_axis=0, concat_axis=0, tiled=True)
    up = lax.ppermute(up, "lat", [(i, i + 1) for i in range(N_LAT - 1)])
    dn = lax.ppermute(dn, "lat", [(i + 1, i) for i in range(N_LAT - 1)])
    turned = (LEV, 128, 128)
    w1, w0, v0, here, upper, lower, gain, q1 = call(
        coef_kernel, 1,
        [(turned, ANYWHERE, True)] * 6 + [((1, 128, 128), None, True), ((COEF, 128), None, False)],
        [whole(east.shape), pl.BlockSpec((1, LEV, ROWS, COLS), lambda i: (0, 0, 0, 0)), whole(up.shape), whole(dn.shape)],
        [(turned, F32)] * 6 + [pltpu.SemaphoreType.DMA((LEV // GROUP, 6)),
         ((LEV, 32, COLS), F32), ((LEV, 32, COLS), F32), ((ABREAST, 3, 128, 128), F32)],
        "coef", 16, pl.CostEstimate(flops=2 * 10**8, transcendentals=0, bytes_accessed=6 * 10**7),
    )(east, north, up, dn)
    tiles = (TR * LEV, 128, 128)
    send2, y, f, rest = call(
        state_kernel, 1,
        [((N_LON, PAYLOAD, 128), None, False), (tiles, None, False), ((TR, ROWS, COLS), None, False),
         ((TR, 128, 128), None, False)],
        [whole((SLOTS, 128)), whole(north.shape), whole(up.shape), whole(dn.shape)] + [ANYWHERE] * 3 + [whole(q1.shape)],
        [(turned, F32)] * 3 + [pltpu.SemaphoreType.DMA((3,)),
         ((128, SLOTS), F32), ((TR * LEV, PAD, COLS), F32), ((TR * LEV, PAD, COLS), F32),
         ((STEPS, LEV, PAD, COLS), F32), ((2, 2, TR, LEV, COLS), F32), ((REST, 128), F32), ((4, 128, 128), F32),
         ((STEPS, TR, 2, LEV, SLOTS), F32), ((2, 16 * HALF, SLOTS), BF16), ((STEPS, HALF, SLOTS), BF16),
         ((STEPS, SLOTS, 2 * COLS), BF16)],
        "state", 32,
    )(recv.reshape(SLOTS, 128), north, up, dn, *in_hbm(w1, w0, v0), q1)
    recv2 = lax.all_to_all(send2, "lon", split_axis=0, concat_axis=0, tiled=True)
    adjoint, flux = call(
        final_kernel, 1,
        [((TR, LEV, ROWS, COLS), ANYWHERE, True), ((TR, ROWS, COLS), None, True)],
        [whole(recv2.shape), whole(tiles)] + [whole(turned)] * 4 + [whole(gain.shape), whole(rest.shape), whole(f.shape)],
        [((TR, LEV, ROWS, COLS), F32), pltpu.SemaphoreType.DMA((LEV // GROUP, TR)), ((N_LON, LEV, 128), F32),
         ((N_LON, TR * LEV, 128), F32), ((N_LON, TR * LEV, 128), F32), ((4, TR * LEV, 128), F32),
         ((TR * FINAL_ABREAST, 128, 128), F32)],
        "final", 24,
    )(recv2, y, here, upper, lower, w0, gain, rest, f)
    return adjoint, flux


def solution(mesh):
    return jax.shard_map(
        shards,
        mesh=mesh,
        in_specs=(
            P(None, None, "lat", "lon"),
            P(None, None, "lat", "lon"),
            P(None, None, ("lat", "lon")),
            P(None, None, ("lat", "lon")),
            P(None, ("lat", "lon")),
            P(None, ("lat", "lon")),
        ),
        out_specs=(P(None, None, "lat", "lon"), P(None, "lat", "lon")),
        check_vma=False,
    )
```

```python
import jax
import jax.numpy as jnp
from jax import lax
from jax.experimental import pallas as pl
from jax.experimental.pallas import tpu as pltpu
from jax.sharding import PartitionSpec as P

F32 = jnp.float32
BF16 = jnp.bfloat16
STEPS, TR, LEV, ROWS, COLS = 2, 2, 16, 96, 128
SLOTS = 1024
N_LAT, N_LON = 8, 16
PAD = 112
TOP = 8
END = TOP + ROWS
HALF = ROWS // 2
FIELDS = 40
COEF = 5 * LEV
REST = 4 * LEV
PAYLOAD = 7 * LEV
GROUP = 4
ABREAST = 8
FINAL_ABREAST = 8
CHUNK = 16
MEGA = 1024 * 1024


def iota(shape, dim):
    return lax.broadcasted_iota(jnp.int32, shape, dim)


def row_ahead(x):
    return pltpu.roll(x, 127, 1)


def row_behind(x):
    return pltpu.roll(x, 1, 1)


def chunk_ahead(x, k):
    return pltpu.roll(x, 8 - k, 0)


def column(m):
    return pl.ds(m, 8, stride=CHUNK)


def register(m):
    return slice(8 * m, 8 * m + 8)


BACKWARD = range(CHUNK - 1, -1, -1)


def step(retain, later, value=None):
    if later is None:
        return value if value is not None else retain
    return value + retain * later if value is not None else retain * later


def chunk_ladders(products):
    last = iota((8, 128), 0) == 7
    values = [jnp.where(last, 0.0, chunk_ahead(x, 1)) for x in products]
    steps = [values]
    for k in (1, 2):
        values = [x * chunk_ahead(x, k) for x in values]
        steps.append(values)
    return steps


def chunk_inflows(steps, firsts, inflows, of):
    last = iota((8, 128), 0) == 7
    values = [jnp.where(last, inflow, chunk_ahead(first, 1)) for first, inflow in zip(firsts, inflows)]
    for k, products in zip((1, 2, 4), steps):
        values = [x + products[i] * chunk_ahead(x, k) for x, i in zip(values, of)]
    return values


def load_columns(ref):
    return [ref[pl.ds(m, 8, stride=CHUNK), :] for m in range(CHUNK)]


def store_registers(ref, lead, values):
    for m in range(CHUNK):
        ref[lead, 8 * m:8 * m + 8, :] = values[m]


def suffix(values, retain):
    out = [None] * CHUNK
    out[-1] = values[-1]
    for m in range(CHUNK - 2, -1, -1):
        out[m] = values[m] + retain[m] * out[m + 1]
    return out


def suffix_product(retain):
    out = [None] * CHUNK
    out[-1] = retain[-1]
    for m in range(CHUNK - 2, -1, -1):
        out[m] = retain[m] * out[m + 1]
    return out


def chunk_ladder(product):
    last = iota(product.shape, 0) == 7
    steps = []
    value = jnp.where(last, 0.0, chunk_ahead(product, 1))
    for k in (1, 2, 4):
        steps.append((k, value))
        if k < 4:
            value = value * chunk_ahead(value, k)
    return steps


def chunk_inflow(steps, first, inflow):
    value = jnp.where(iota(first.shape, 0) == 7, inflow, chunk_ahead(first, 1))
    for k, product in steps:
        value = value + product * chunk_ahead(value, k)
    return value


def masked_north(v, is_top):
    return jnp.where((iota(v.shape, 0) == ROWS - 1) & is_top, 0.0, v)


def top_flag():
    return lax.axis_index("lat") == N_LAT - 1


def pack_kernel(ker_hbm, dep_hbm, cell_hbm, cnt_hbm, north_hbm, east_hbm,
                send_hbm, up_ref, dn_ref,
                ker_ref, dep_ref, cell_ref, cnt_ref, nlast_ref, nfirst_ref, elast_ref, efirst_ref, x_ref, send_ref, sems, out_sems):
    copies = [
        pltpu.make_async_copy(cnt_hbm, cnt_ref, sems.at[0]),
        pltpu.make_async_copy(dep_hbm, dep_ref, sems.at[1]),
        pltpu.make_async_copy(cell_hbm, cell_ref, sems.at[2]),
        pltpu.make_async_copy(ker_hbm, ker_ref, sems.at[3]),
        pltpu.make_async_copy(north_hbm.at[:, :, ROWS - 8:, :], nlast_ref, sems.at[4]),
        pltpu.make_async_copy(north_hbm.at[1, :, :8, :], nfirst_ref, sems.at[5]),
        pltpu.make_async_copy(east_hbm.at[1, :, ROWS - 8:, :], elast_ref, sems.at[6]),
        pltpu.make_async_copy(east_hbm.at[1, :, :8, :], efirst_ref, sems.at[7]),
    ]
    for copy in copies:
        copy.start()
    spread = jnp.where(iota((128, SLOTS), 1) // 8 == iota((128, SLOTS), 0), 1.0, 0.0).astype(BF16)
    within = (iota((8, SLOTS), 1) % 8).astype(F32)
    for copy in copies[:4]:
        copy.wait()
    for n in range(STEPS):
        x_ref[n * LEV:(n + 1) * LEV, :] = ker_ref[n]
    counts = jnp.concatenate([cnt_ref[...].astype(F32), jnp.zeros((6, 128), F32)], axis=0)
    counts = jnp.dot(counts.astype(BF16), spread, preferred_element_type=F32)
    live = jnp.where(within < counts, 1.0, 0.0)
    rows = []
    for n in range(STEPS):
        rows.append(dep_ref[n] * live[n:n + 1])
    rows.append(cell_ref[...].astype(F32))
    rows.append(jnp.zeros((2, SLOTS), F32))
    x_ref[2 * LEV:FIELDS, :] = jnp.concatenate(rows, axis=0)
    none = jnp.zeros((FIELDS, 128), F32)

    def lanes(b):
        if b < 0 or b >= N_LAT:
            return none
        return x_ref[:, b * 128:(b + 1) * 128]

    outs = []
    for b in range(N_LAT):
        tile = jnp.concatenate([lanes(b), lanes(b - 1), lanes(b + 1), jnp.zeros((8, 128), F32)], axis=0)
        block = pl.ds(b * 128, 128)
        send_ref[b * 128:(b + 1) * 128, :] = tile.T
        outs.append(pltpu.make_async_copy(send_ref.at[block], send_hbm.at[block], out_sems.at[b]))
        outs[-1].start()
    for copy in copies[4:]:
        copy.wait()
    up_ref[0] = nlast_ref[0, :, 7, :]
    up_ref[1] = nlast_ref[1, :, 6, :]
    up_ref[2] = nlast_ref[1, :, 7, :]
    up_ref[3] = elast_ref[:, 7, :]
    dn_ref[0] = nfirst_ref[:, 0, :]
    dn_ref[1] = efirst_ref[:, 0, :]
    for copy in outs:
        copy.wait()


def coef_kernel(east_ref, north_ref, up_ref, dn_ref,
                w1_hbm, w0_hbm, here_hbm, upper_hbm, lower_hbm, gain_ref, q_ref,
                w1_ref, w0_ref, here_ref, upper_ref, lower_ref, sems,
                he_ref, hv_ref, t_ref):
    is_top = top_flag()
    he_ref[...] = jnp.zeros(he_ref.shape, F32)
    hv_ref[...] = jnp.zeros(hv_ref.shape, F32)
    for lev in range(LEV):
        he_ref[lev, 0:1, :] = dn_ref[1, lev:lev + 1, :]
        he_ref[lev, 31:32, :] = up_ref[3, lev:lev + 1, :]
        hv_ref[lev, 31:32, :] = up_ref[0, lev:lev + 1, :]
    outs = ((w1_ref, w1_hbm), (w0_ref, w0_hbm), (here_ref, here_hbm), (upper_ref, upper_hbm),
            (lower_ref, lower_hbm))

    def level(lev, slot):
        t_ref[slot, 0] = jnp.concatenate([east_ref[1, lev], he_ref[lev]], axis=0).T
        t_ref[slot, 1] = jnp.concatenate([east_ref[0, lev], jnp.zeros((32, COLS), F32)], axis=0).T
        t_ref[slot, 2] = jnp.concatenate([masked_north(north_ref[0, lev], is_top), hv_ref[lev]], axis=0).T
        one = jnp.ones((8, 128), F32)
        none = jnp.zeros((8, 128), F32)
        w1 = [1.0 / (1.0 + c) for c in load_columns(t_ref.at[slot, 0])]
        store_registers(w1_ref, lev, w1)
        product = suffix_product([1.0 - w for w in w1])
        ends = chunk_inflow(chunk_ladder(product[0]), none, one)
        gain = [d * ends for d in product]
        q_ref[lev:lev + 1, :] = gain[0][0:1]

        if lev == 0:
            store_registers(gain_ref, 0, gain)


        w0 = [1.0 / (1.0 + c) for c in load_columns(t_ref.at[slot, 1])]
        store_registers(w0_ref, lev, w0)
        r0 = [1.0 - w for w in w0]
        product = suffix_product(r0)
        steps = chunk_ladder(product[0])
        q_ref[lev + 4 * LEV:lev + 4 * LEV + 1, :] = (product[0] * chunk_inflow(steps, none, one))[0:1]
        v = load_columns(t_ref.at[slot, 2])
        rows = range(CHUNK)
        north = [jnp.maximum(x, 0.0) for x in v]
        south = [jnp.minimum(x, 0.0) for x in v]
        beyond = [row_ahead(x) for x in gain]
        here = [w0[m] * ((1.0 - north[m]) * gain[m] + row_behind(south[m] * beyond[m])) for m in rows]
        upper = [w0[m] * north[m] * beyond[m] for m in rows]
        lower = [-w0[m] * row_behind(south[m] * gain[m]) for m in rows]
        for k, (ref, values) in enumerate(((here_ref, here), (upper_ref, upper), (lower_ref, lower))):
            store_registers(ref, lev, values)
            first = suffix(values, r0)[0]
            total = first + product[0] * chunk_inflow(steps, first, none)
            q_ref[lev + (k + 1) * LEV:lev + (k + 1) * LEV + 1, :] = total[0:1]

    copies = []
    for g in range(LEV // GROUP):
        for lev in range(g * GROUP, (g + 1) * GROUP):
            level(lev, lev % ABREAST)
        for i, (source, target) in enumerate(outs):
            part = pl.ds(g * GROUP, GROUP)
            copies.append(pltpu.make_async_copy(source.at[part], target.at[part], sems.at[g, i]))
            copies[-1].start()
    for copy in copies:
        copy.wait()


def split(x):
    high = x.astype(BF16).astype(F32)
    return high, x - high


def product_nt(a, b):
    return lax.dot_general(a, b, (((1,), (1,)), ((), ())), preferred_element_type=F32)


def state_kernel(recv_ref, north_ref, up_ref, dn_ref, w1_hbm, w0_hbm, q1_ref,
                 send_ref, y_ref, flux_ref,
                 w1_ref, w0_ref, in_sems, x_ref, f1_ref, f0_ref, v_ref, e_ref, q_ref, t_ref, t2_ref, u_ref, p_ref, b_ref, term_ref, lhs_ref, mask_ref, hot_ref):
    is_top = top_flag()
    fetches = [
        pltpu.make_async_copy(source, target, in_sems.at[i])
        for i, (source, target) in enumerate(
            ((w1_hbm, w1_ref), (w0_hbm, w0_ref)))
    ]
    for fetch in fetches:
        fetch.start()
    for b in range(N_LAT):
        x_ref[:, b * 128:(b + 1) * 128] = recv_ref[b * 128:(b + 1) * 128, :].T

    def place(offset, n):
        cell = x_ref[offset + 36 + n:offset + 37 + n, :].astype(jnp.int32)
        return cell >> 7, cell & 127

    def make_terms(offset, n):
        parts = []
        for t in range(TR):
            value = x_ref[offset + 32 + 2 * n + t:offset + 33 + 2 * n + t, :]
            parts.append(split(value * x_ref[offset + n * LEV:offset + (n + 1) * LEV, :]))
        return parts

    for n in (1, 0):
        parts = make_terms(0, n)
        for t in range(TR):
            for p in range(2):
                term_ref[n, t, p] = parts[t][p]
        row, _ = place(0, n)
        later = row >= HALF
        row = jnp.where(later, row - HALF, row)
        mask_ref[n] = jnp.where(iota((HALF, SLOTS), 0) == row, 1.0, 0.0).astype(BF16)
        cell = recv_ref[:, 36 + n:37 + n].astype(jnp.int32)
        col = (cell & 127) + jnp.where(cell >= HALF * COLS, COLS, 0)
        hot_ref[n] = jnp.where(iota((SLOTS, 2 * COLS), 1) == col, 1.0, 0.0).astype(BF16)

    def deposit(g):
        for n in (1, 0):
            target = (f0_ref, f1_ref)[n]
            for i in range(GROUP):
                for t in range(TR):
                    for p in range(2):
                        at = ((i * TR + t) * 2 + p) * HALF
                        term = term_ref[n, t, p, g * GROUP + i:g * GROUP + i + 1, :]
                        term = jnp.broadcast_to(term, (16, SLOTS)).astype(BF16)
                        lhs_ref[n, at:at + HALF, :] = mask_ref[n] * jnp.concatenate([term] * 3, axis=0)
            out = jnp.dot(lhs_ref[n], hot_ref[n], preferred_element_type=F32)
            for i in range(GROUP):
                for t in range(TR):
                    at = (i * TR + t) * 2 * HALF
                    both = out[at:at + HALF] + out[at + HALF:at + 2 * HALF]
                    target[t * LEV + g * GROUP + i, TOP:TOP + HALF, :] = both[:, :COLS]
                    target[t * LEV + g * GROUP + i, TOP + HALF:END, :] = both[:, COLS:]

    edges = {}
    for side, offset in ((0, FIELDS), (1, 2 * FIELDS)):
        for n in (1, 0):
            rows = ((ROWS - 1, ROWS - 2), (0, 1))[side][:2 if n else 1]
            row, col = place(offset, n)
            hot = jnp.where(iota((COLS, SLOTS), 0) == col, 1.0, 0.0).astype(BF16)
            parts = make_terms(offset, n)
            stack = []
            for r in rows:
                hit = jnp.where(row == r, 1.0, 0.0)
                for t in range(TR):
                    for p in range(2):
                        stack.append((parts[t][p] * hit).astype(BF16))
            out = product_nt(jnp.concatenate(stack, axis=0), hot)
            for i in range(len(rows)):
                for t in range(TR):
                    at = (i * TR + t) * 2 * LEV
                    edges[side, n, i, t] = out[at:at + LEV] + out[at + LEV:at + 2 * LEV]

    for (side, n, i, t), value in edges.items():
        if n == 1:
            e_ref[side, i, t] = value
        if i == 0:
            where = iota((8, COLS), 0) == (7 if side == 0 else 0)
            at = 0 if side == 0 else END
            for lev in range(LEV):
                (f0_ref, f1_ref)[n][t * LEV + lev, at:at + 8, :] = jnp.where(where, value[lev:lev + 1, :], 0.0)
    for lev in range(LEV):
        v_ref[1, lev, TOP - 1:TOP, :] = up_ref[2, lev:lev + 1, :]
        v_ref[0, lev, TOP - 1:TOP, :] = up_ref[0, lev:lev + 1, :]
    low_north = jnp.maximum(up_ref[2], 0.0)
    low_south = jnp.minimum(up_ref[1], 0.0)
    high_north = jnp.maximum(dn_ref[0], 0.0)
    high_south = jnp.minimum(jnp.where(is_top, 0.0, north_ref[1, :, ROWS - 1, :]), 0.0)
    deposit(0)
    for fetch in fetches:
        fetch.wait()

    def edge_rows(lev, t):
        at = t * LEV + lev
        one = slice(lev, lev + 1)
        low, below = e_ref[0, 0, t, one, :], e_ref[0, 1, t, one, :]
        low = low + low_north[one] * (f1_ref[at, TOP:TOP + 1, :] - low) + low_south[one] * (low - below)
        high, above = e_ref[1, 0, t, one, :], e_ref[1, 1, t, one, :]
        high = high + high_north[one] * (above - high) + high_south[one] * (high - f1_ref[at, END - 1:END, :])
        row = iota((32, COLS), 0)
        return jnp.where(row == 0, high, jnp.where(row == 31, low, 0.0))

    none = jnp.zeros((8, 128), F32)
    below = jnp.zeros((32, COLS), F32)

    def transported(ref, n, lev, at):
        north = jnp.maximum(v_ref[n, lev, TOP:END, :], 0.0)
        south = jnp.minimum(v_ref[n, lev, TOP - 1:END - 1, :], 0.0)
        a = ref[at, TOP:END, :]
        return a + north * (ref[at, TOP + 1:END + 1, :] - a) + south * (a - ref[at, TOP - 1:END - 1, :])

    def latitude1(lev, slot):
        for n in range(STEPS):
            v_ref[n, lev, TOP:END, :] = masked_north(north_ref[n, lev], is_top)
        for t in range(TR):
            t_ref[slot + t] = jnp.concatenate([transported(f1_ref, 1, lev, t * LEV + lev), edge_rows(lev, t)], axis=0).T

    def longitude1(levels):
        ends, firsts = [], []
        for lev in levels:
            slot = TR * (lev % ABREAST)
            product, later = None, [None] * TR
            for m in BACKWARD:
                w = w1_ref[lev, register(m), :]
                r = 1.0 - w
                product = step(r, product)
                p_ref[lev % ABREAST, register(m), :] = product
                for t in range(TR):
                    later[t] = step(r, later[t], w * t_ref[slot + t, column(m), :])
                    t2_ref[slot + t, register(m), :] = later[t]
            ends.append(product)
            firsts += later
        of = [i for i in range(len(levels)) for _ in range(TR)]
        enter = chunk_inflows(chunk_ladders(ends), firsts, [none] * len(firsts), of)
        for i, lev in enumerate(levels):
            slot = TR * (lev % ABREAST)
            for m in range(CHUNK):
                product = p_ref[lev % ABREAST, register(m), :]
                for t in range(TR):
                    rest = t2_ref[slot + t, register(m), :] + product * enter[TR * i + t]
                    if m == 0:
                        at = t * LEV + lev
                        q_ref[at:at + 1, :] = rest[0:1]
                    u_ref[slot + t, column(m), :] = rest

    def latitude0(lev, slot):
        for t in range(TR):
            at = t * LEV + lev
            rest = u_ref[slot + t].T
            b_ref[slot + t, TOP:END, :] = f0_ref[at, TOP:END, :] + rest[0:ROWS]
            b_ref[slot + t, 0:TOP, :] = f0_ref[at, 0:TOP, :] + rest[120:128]
            b_ref[slot + t, END:PAD, :] = f0_ref[at, END:PAD, :] + rest[ROWS:ROWS + 8]
            if lev == 0:
                flux_ref[t] = f1_ref[at, TOP:END, :] + b_ref[slot + t, TOP:END, :]
            t_ref[slot + t] = jnp.concatenate([transported(b_ref, 0, lev, slot + t), below], axis=0).T

    def longitude0(levels):
        ends, firsts = [], []
        for lev in levels:
            slot = TR * (lev % ABREAST)
            product, later = None, [None] * TR
            for m in BACKWARD:
                w = w0_ref[lev, register(m), :]
                r = 1.0 - w
                product = step(r, product)
                for t in range(TR):
                    value = w * t_ref[slot + t, column(m), :]
                    y_ref[t * LEV + lev, register(m), :] = value
                    later[t] = step(r, later[t], value)
            ends.append(product)
            firsts += later
        of = [i for i in range(len(levels)) for _ in range(TR)]
        enter = chunk_inflows(chunk_ladders(ends), firsts, [none] * len(firsts), of)
        for i, lev in enumerate(levels):
            for t in range(TR):
                total = firsts[TR * i + t] + ends[i] * enter[TR * i + t]
                at = TR * LEV + t * LEV + lev
                q_ref[at:at + 1, :] = total[0:1]

    for g in range(LEV // GROUP):
        if g + 1 < LEV // GROUP:
            deposit(g + 1)
        levels = range(g * GROUP, (g + 1) * GROUP)
        for lev in levels:
            latitude1(lev, TR * (lev % ABREAST))
        longitude1(levels)
        for lev in levels:
            latitude0(lev, TR * (lev % ABREAST))
        longitude0(levels)
    q1 = q1_ref[...]
    gamma, gain0 = q1[3 * LEV:4 * LEV], q1[4 * LEV:]
    lane = iota((LEV, 128), 1)
    rows = []
    bases = [q_ref[i * LEV:(i + 1) * LEV, :] for i in range(4)] + [q1[LEV:2 * LEV], q1[0:LEV], q1[2 * LEV:3 * LEV]]
    riders = [(gain0, 65), (gain0, 35), (gamma, 96), (gamma, 64), (gamma, 32), (gain0, 5), (gain0, 96)]
    for i, (base, (rider, shift)) in enumerate(zip(bases, riders)):
        spare = (lane > ROWS) & (lane < 127) if i in (0, 1, 5) else lane >= ROWS
        rows.append(jnp.where(spare, pltpu.roll(rider, shift, 1), base))
    payload = jnp.concatenate(rows, axis=0)
    for j in range(N_LON):
        send_ref[j] = payload


def final_kernel(recv_ref, y_ref, here_ref, upper_ref, lower_ref, w0_ref, gain_ref, f_ref,
                 adj_hbm, flux_ref, adj_ref, sems, gamma_ref, gain0_ref, in1_ref, in0_ref, flow_ref, t_ref, u_ref, p_ref):
    me = lax.axis_index("lon")

    def part(j, i):
        return recv_ref[j, i * LEV:(i + 1) * LEV, :]

    lane = iota((LEV, 128), 1)

    def gamma(j):
        first, second, third = (pltpu.roll(part(j, 2 + i), 32 * (i + 1), 1) for i in range(3))
        return jnp.where(lane < 32, first, jnp.where(lane < 64, second, third))

    def gain0(j):
        pieces = [pltpu.roll(part(j, i), shift, 1) for i, shift in ((6, 32), (0, 63), (1, 93), (5, 123))]
        return jnp.where(lane < 32, pieces[0],
                         jnp.where(lane < 62, pieces[1], jnp.where(lane < 92, pieces[2], pieces[3])))

    for j in range(N_LON):
        gamma_ref[j] = gamma(j)
        gain0_ref[j] = gain0(j)

    def both(x):
        return jnp.concatenate([x, x], axis=0)

    pair = (TR * LEV, 128)
    gain = jnp.ones((LEV, 128), F32)
    rest = jnp.zeros(pair, F32)
    for j in range(N_LON - 1, -1, -1):
        g = part(j, 5)
        rest = both(g) * rest + recv_ref[j, 0:TR * LEV, :]
        gain = g * gain
    inflow = rest * both(1.0 / (1.0 - gain))
    gain = jnp.ones((LEV, 128), F32)
    rest = jnp.zeros(pair, F32)
    for j in range(N_LON - 1, -1, -1):
        in1_ref[j] = inflow
        total = recv_ref[j, TR * LEV:2 * TR * LEV, :] + both(part(j, 4)) * inflow
        total = total + both(part(j, 6)) * row_ahead(inflow) + both(gamma_ref[j]) * row_behind(inflow)
        in0_ref[j] = total
        inflow = both(part(j, 5)) * inflow + recv_ref[j, 0:TR * LEV, :]
        g = gain0_ref[j]
        rest = both(g) * rest + total
        gain = g * gain
    inflow = rest * both(1.0 / (1.0 - gain))
    for j in range(N_LON - 1, -1, -1):
        total = in0_ref[j]
        in0_ref[j] = inflow
        inflow = both(gain0_ref[j]) * inflow + total
    mine = in1_ref[me]
    flow_ref[0] = mine
    flow_ref[1] = row_ahead(mine)
    flow_ref[2] = row_behind(mine)
    flow_ref[3] = in0_ref[me]

    for t in range(TR):
        flow = flow_ref[0, t * LEV:t * LEV + 1, :]
        for m in range(CHUNK):
            t_ref[t, column(m), :] = gain_ref[0, register(m), :] * flow
        flux_ref[t] = f_ref[t] + t_ref[t].T[0:ROWS]

    def longitude0(levels):
        ends, firsts, inflows = [], [], []
        for lev in levels:
            product, later = None, [None] * TR
            flows = [[flow_ref[i, t * LEV + lev:t * LEV + lev + 1, :] for i in range(4)] for t in range(TR)]
            for m in BACKWARD:
                r = 1.0 - w0_ref[lev, register(m), :]
                product = step(r, product)
                p_ref[lev % FINAL_ABREAST, register(m), :] = product
                here, upper, lower = (ref[lev, register(m), :] for ref in (here_ref, upper_ref, lower_ref))
                for t in range(TR):
                    at = t * LEV + lev
                    value = y_ref[at, register(m), :] + here * flows[t][0] + upper * flows[t][1] + lower * flows[t][2]
                    later[t] = step(r, later[t], value)
                    u_ref[TR * (lev % FINAL_ABREAST) + t, register(m), :] = later[t]
            ends.append(product)
            firsts += later
            inflows += [flows[t][3] for t in range(TR)]
        of = [i for i in range(len(levels)) for _ in range(TR)]
        enter = chunk_inflows(chunk_ladders(ends), firsts, inflows, of)
        for i, lev in enumerate(levels):
            for t in range(TR):
                slot = TR * (lev % FINAL_ABREAST) + t
                for m in range(CHUNK):
                    value = u_ref[slot, register(m), :]
                    value = value + p_ref[lev % FINAL_ABREAST, register(m), :] * enter[TR * i + t]
                    t_ref[slot, column(m), :] = value
                adj_ref[t, lev] = t_ref[slot].T[0:ROWS]

    copies = []
    for g in range(LEV // GROUP):
        longitude0(range(g * GROUP, (g + 1) * GROUP))
        for t in range(TR):
            part_of = pl.ds(g * GROUP, GROUP)
            copies.append(pltpu.make_async_copy(adj_ref.at[t, part_of], adj_hbm.at[t, part_of], sems.at[g, t]))
            copies[-1].start()
    for copy in copies:
        copy.wait()


def whole(shape):
    return pl.BlockSpec(shape, lambda i: (0,) * len(shape))


def in_hbm(*arrays):
    return [pltpu.with_memory_space_constraint(x, pltpu.HBM) for x in arrays]


ANYWHERE = pl.BlockSpec(memory_space=pltpu.HBM)


def call(kernel, steps, outs, in_specs, scratch, name, mega, cost=None):
    return pl.pallas_call(
        kernel,
        grid=(steps,),
        out_shape=[pltpu.HBM(s, F32) if hbm else jax.ShapeDtypeStruct(s, F32) for s, _, hbm in outs],
        in_specs=in_specs,
        out_specs=[whole(s) if spec is None else spec for s, spec, _ in outs],
        scratch_shapes=[pltpu.VMEM(*s) if isinstance(s, tuple) else s for s in scratch],
        compiler_params=pltpu.CompilerParams(vmem_limit_bytes=mega * MEGA),
        cost_estimate=cost,
        name=name,
    )


def shards(east, north, kernels, departures, cells, counts):
    send, up, dn = call(
        pack_kernel, 1,
        [((SLOTS, 128), ANYWHERE, True), ((4, LEV, COLS), None, False), ((2, LEV, COLS), None, False)],
        [ANYWHERE] * 6,
        [(kernels.shape, F32), (departures.shape, F32), (cells.shape, jnp.int32), (counts.shape, jnp.int32),
         ((STEPS, LEV, 8, COLS), F32), ((LEV, 8, COLS), F32), ((LEV, 8, COLS), F32), ((LEV, 8, COLS), F32),
         ((FIELDS, SLOTS), F32), ((SLOTS, 128), F32), pltpu.SemaphoreType.DMA((8,)),
         pltpu.SemaphoreType.DMA((N_LAT,))],
        "pack", 8,
    )(*in_hbm(kernels, departures, cells, counts, north, east))
    recv = lax.all_to_all(send.reshape(128, 8, 128), ("lat", "lon"), split_axis=0, concat_axis=0, tiled=True)
    up = lax.ppermute(up, "lat", [(i, i + 1) for i in range(N_LAT - 1)])
    dn = lax.ppermute(dn, "lat", [(i + 1, i) for i in range(N_LAT - 1)])
    turned = (LEV, 128, 128)
    w1, w0, here, upper, lower, gain, q1 = call(
        coef_kernel, 1,
        [(turned, ANYWHERE, True)] * 5 + [((1, 128, 128), None, True), ((COEF, 128), None, False)],
        [whole(east.shape), pl.BlockSpec((1, LEV, ROWS, COLS), lambda i: (0, 0, 0, 0)), whole(up.shape), whole(dn.shape)],
        [(turned, F32)] * 5 + [pltpu.SemaphoreType.DMA((LEV // GROUP, 5)),
         ((LEV, 32, COLS), F32), ((LEV, 32, COLS), F32), ((ABREAST, 3, 128, 128), F32)],
        "coef", 16, pl.CostEstimate(flops=2 * 10**8, transcendentals=0, bytes_accessed=6 * 10**7),
    )(east, north, up, dn)
    tiles = (TR * LEV, 128, 128)
    send2, y, f = call(
        state_kernel, 1,
        [((N_LON, PAYLOAD, 128), None, False), (tiles, None, False), ((TR, ROWS, COLS), None, False)],
        [whole((SLOTS, 128)), whole(north.shape), whole(up.shape), whole(dn.shape)] + [ANYWHERE] * 2 + [whole(q1.shape)],
        [(turned, F32)] * 2 + [pltpu.SemaphoreType.DMA((2,)),
         ((128, SLOTS), F32), ((TR * LEV, PAD, COLS), F32), ((TR * LEV, PAD, COLS), F32),
         ((STEPS, LEV, PAD, COLS), F32), ((2, 2, TR, LEV, COLS), F32), ((REST, 128), F32),
         ((TR * ABREAST, 128, 128), F32), ((TR * ABREAST, 128, 128), F32), ((TR * ABREAST, 128, 128), F32),
         ((ABREAST, 128, 128), F32), ((TR * ABREAST, PAD, COLS), F32), ((STEPS, TR, 2, LEV, SLOTS), F32), ((2, 16 * HALF, SLOTS), BF16), ((STEPS, HALF, SLOTS), BF16),
         ((STEPS, SLOTS, 2 * COLS), BF16)],
        "state", 32,
    )(recv.reshape(SLOTS, 128), north, up, dn, *in_hbm(w1, w0), q1)
    recv2 = lax.all_to_all(send2, "lon", split_axis=0, concat_axis=0, tiled=True)
    adjoint, flux = call(
        final_kernel, 1,
        [((TR, LEV, ROWS, COLS), ANYWHERE, True), ((TR, ROWS, COLS), None, True)],
        [whole(recv2.shape), whole(tiles)] + [whole(turned)] * 4 + [whole(gain.shape), whole(f.shape)],
        [((TR, LEV, ROWS, COLS), F32), pltpu.SemaphoreType.DMA((LEV // GROUP, TR)), ((N_LON, LEV, 128), F32),
         ((N_LON, LEV, 128), F32), ((N_LON, TR * LEV, 128), F32), ((N_LON, TR * LEV, 128), F32), ((4, TR * LEV, 128), F32),
         ((TR * FINAL_ABREAST, 128, 128), F32), ((TR * FINAL_ABREAST, 128, 128), F32),
         ((FINAL_ABREAST, 128, 128), F32)],
        "final", 24,
    )(recv2, y, here, upper, lower, w0, gain, f)
    return adjoint, flux


def solution(mesh):
    return jax.shard_map(
        shards,
        mesh=mesh,
        in_specs=(
            P(None, None, "lat", "lon"),
            P(None, None, "lat", "lon"),
            P(None, None, ("lat", "lon")),
            P(None, None, ("lat", "lon")),
            P(None, ("lat", "lon")),
            P(None, ("lat", "lon")),
        ),
        out_specs=(P(None, None, "lat", "lon"), P(None, "lat", "lon")),
        check_vma=False,
    )
```

```python
import jax
import jax.numpy as jnp
from jax import lax
from jax.experimental import pallas as pl
from jax.experimental.pallas import tpu as pltpu
from jax.sharding import PartitionSpec as P

F32 = jnp.float32
BF16 = jnp.bfloat16
STEPS, TR, LEV, ROWS, COLS = 2, 2, 16, 96, 128
SLOTS = 1024
N_LAT, N_LON = 8, 16
PAD = 112
TOP = 8
END = TOP + ROWS
HALF = ROWS // 2
FIELDS = 40
COEF = 5 * LEV
REST = 4 * LEV
PAYLOAD = 7 * LEV
GROUP = 4
ABREAST = 8
FINAL_ABREAST = 8
CHUNK = 16
MEGA = 1024 * 1024


def iota(shape, dim):
    return lax.broadcasted_iota(jnp.int32, shape, dim)


def row_ahead(x):
    return pltpu.roll(x, 127, 1)


def row_behind(x):
    return pltpu.roll(x, 1, 1)


def chunk_ahead(x, k):
    return pltpu.roll(x, 8 - k, 0)


def column(m):
    return pl.ds(m, 8, stride=CHUNK)


def register(m):
    return slice(8 * m, 8 * m + 8)


BACKWARD = range(CHUNK - 1, -1, -1)


def step(retain, later, value=None):
    if later is None:
        return value if value is not None else retain
    return value + retain * later if value is not None else retain * later


def chunk_ladders(products):
    last = iota((8, 128), 0) == 7
    values = [jnp.where(last, 0.0, chunk_ahead(x, 1)) for x in products]
    steps = [values]
    for k in (1, 2):
        values = [x * chunk_ahead(x, k) for x in values]
        steps.append(values)
    return steps


def chunk_inflows(steps, firsts, inflows, of):
    last = iota((8, 128), 0) == 7
    values = [jnp.where(last, inflow, chunk_ahead(first, 1)) for first, inflow in zip(firsts, inflows)]
    for k, products in zip((1, 2, 4), steps):
        values = [x + products[i] * chunk_ahead(x, k) for x, i in zip(values, of)]
    return values


def load_columns(ref):
    return [ref[pl.ds(m, 8, stride=CHUNK), :] for m in range(CHUNK)]


def store_registers(ref, lead, values):
    for m in range(CHUNK):
        ref[lead, 8 * m:8 * m + 8, :] = values[m]


def suffix(values, retain):
    out = [None] * CHUNK
    out[-1] = values[-1]
    for m in range(CHUNK - 2, -1, -1):
        out[m] = values[m] + retain[m] * out[m + 1]
    return out


def suffix_product(retain):
    out = [None] * CHUNK
    out[-1] = retain[-1]
    for m in range(CHUNK - 2, -1, -1):
        out[m] = retain[m] * out[m + 1]
    return out


def chunk_ladder(product):
    last = iota(product.shape, 0) == 7
    steps = []
    value = jnp.where(last, 0.0, chunk_ahead(product, 1))
    for k in (1, 2, 4):
        steps.append((k, value))
        if k < 4:
            value = value * chunk_ahead(value, k)
    return steps


def chunk_inflow(steps, first, inflow):
    value = jnp.where(iota(first.shape, 0) == 7, inflow, chunk_ahead(first, 1))
    for k, product in steps:
        value = value + product * chunk_ahead(value, k)
    return value


def masked_north(v, is_top):
    return jnp.where((iota(v.shape, 0) == ROWS - 1) & is_top, 0.0, v)


def top_flag():
    return lax.axis_index("lat") == N_LAT - 1


def pack_kernel(ker_hbm, dep_hbm, cell_hbm, cnt_hbm, north_hbm, east_hbm,
                send_hbm, up_ref, dn_ref,
                ker_ref, dep_ref, cell_ref, cnt_ref, nlast_ref, nfirst_ref, elast_ref, efirst_ref, x_ref, send_ref, sems, out_sems):
    copies = [
        pltpu.make_async_copy(cnt_hbm, cnt_ref, sems.at[0]),
        pltpu.make_async_copy(dep_hbm, dep_ref, sems.at[1]),
        pltpu.make_async_copy(cell_hbm, cell_ref, sems.at[2]),
        pltpu.make_async_copy(ker_hbm, ker_ref, sems.at[3]),
        pltpu.make_async_copy(north_hbm.at[:, :, ROWS - 8:, :], nlast_ref, sems.at[4]),
        pltpu.make_async_copy(north_hbm.at[1, :, :8, :], nfirst_ref, sems.at[5]),
        pltpu.make_async_copy(east_hbm.at[1, :, ROWS - 8:, :], elast_ref, sems.at[6]),
        pltpu.make_async_copy(east_hbm.at[1, :, :8, :], efirst_ref, sems.at[7]),
    ]
    for copy in copies:
        copy.start()
    spread = jnp.where(iota((128, SLOTS), 1) // 8 == iota((128, SLOTS), 0), 1.0, 0.0).astype(BF16)
    within = (iota((8, SLOTS), 1) % 8).astype(F32)
    for copy in copies[:4]:
        copy.wait()
    for n in range(STEPS):
        x_ref[n * LEV:(n + 1) * LEV, :] = ker_ref[n]
    counts = jnp.concatenate([cnt_ref[...].astype(F32), jnp.zeros((6, 128), F32)], axis=0)
    counts = jnp.dot(counts.astype(BF16), spread, preferred_element_type=F32)
    live = jnp.where(within < counts, 1.0, 0.0)
    rows = []
    for n in range(STEPS):
        rows.append(dep_ref[n] * live[n:n + 1])
    rows.append(cell_ref[...].astype(F32))
    rows.append(jnp.zeros((2, SLOTS), F32))
    x_ref[2 * LEV:FIELDS, :] = jnp.concatenate(rows, axis=0)
    none = jnp.zeros((FIELDS, 128), F32)

    def lanes(b):
        if b < 0 or b >= N_LAT:
            return none
        return x_ref[:, b * 128:(b + 1) * 128]

    outs = []
    for b in range(N_LAT):
        tile = jnp.concatenate([lanes(b), lanes(b - 1), lanes(b + 1), jnp.zeros((8, 128), F32)], axis=0)
        block = pl.ds(b * 128, 128)
        send_ref[b * 128:(b + 1) * 128, :] = tile.T
        outs.append(pltpu.make_async_copy(send_ref.at[block], send_hbm.at[block], out_sems.at[b]))
        outs[-1].start()
    for copy in copies[4:]:
        copy.wait()
    up_ref[0] = nlast_ref[0, :, 7, :]
    up_ref[1] = nlast_ref[1, :, 6, :]
    up_ref[2] = nlast_ref[1, :, 7, :]
    up_ref[3] = elast_ref[:, 7, :]
    dn_ref[0] = nfirst_ref[:, 0, :]
    dn_ref[1] = efirst_ref[:, 0, :]
    for copy in outs:
        copy.wait()


def coef_kernel(east_ref, north_ref, up_ref, dn_ref,
                w1_hbm, w0_hbm, here_hbm, upper_hbm, lower_hbm, gain_ref, q_ref,
                w1_ref, w0_ref, here_ref, upper_ref, lower_ref, sems,
                he_ref, hv_ref, t_ref):
    is_top = top_flag()
    he_ref[...] = jnp.zeros(he_ref.shape, F32)
    hv_ref[...] = jnp.zeros(hv_ref.shape, F32)
    for lev in range(LEV):
        he_ref[lev, 0:1, :] = dn_ref[1, lev:lev + 1, :]
        he_ref[lev, 31:32, :] = up_ref[3, lev:lev + 1, :]
        hv_ref[lev, 31:32, :] = up_ref[0, lev:lev + 1, :]
    outs = ((w1_ref, w1_hbm), (w0_ref, w0_hbm), (here_ref, here_hbm), (upper_ref, upper_hbm),
            (lower_ref, lower_hbm))

    def level(lev, slot):
        t_ref[slot, 0] = jnp.concatenate([east_ref[1, lev], he_ref[lev]], axis=0).T
        t_ref[slot, 1] = jnp.concatenate([east_ref[0, lev], jnp.zeros((32, COLS), F32)], axis=0).T
        t_ref[slot, 2] = jnp.concatenate([masked_north(north_ref[0, lev], is_top), hv_ref[lev]], axis=0).T
        one = jnp.ones((8, 128), F32)
        none = jnp.zeros((8, 128), F32)
        w1 = [1.0 / (1.0 + c) for c in load_columns(t_ref.at[slot, 0])]
        store_registers(w1_ref, lev, w1)
        product = suffix_product([1.0 - w for w in w1])
        ends = chunk_inflow(chunk_ladder(product[0]), none, one)
        gain = [d * ends for d in product]
        q_ref[lev:lev + 1, :] = gain[0][0:1]

        if lev == 0:
            store_registers(gain_ref, 0, gain)


        w0 = [1.0 / (1.0 + c) for c in load_columns(t_ref.at[slot, 1])]
        store_registers(w0_ref, lev, w0)
        r0 = [1.0 - w for w in w0]
        product = suffix_product(r0)
        steps = chunk_ladder(product[0])
        q_ref[lev + 4 * LEV:lev + 4 * LEV + 1, :] = (product[0] * chunk_inflow(steps, none, one))[0:1]
        v = load_columns(t_ref.at[slot, 2])
        rows = range(CHUNK)
        north = [jnp.maximum(x, 0.0) for x in v]
        south = [jnp.minimum(x, 0.0) for x in v]
        beyond = [row_ahead(x) for x in gain]
        here = [w0[m] * ((1.0 - north[m]) * gain[m] + row_behind(south[m] * beyond[m])) for m in rows]
        upper = [w0[m] * north[m] * beyond[m] for m in rows]
        lower = [-w0[m] * row_behind(south[m] * gain[m]) for m in rows]
        for k, (ref, values) in enumerate(((here_ref, here), (upper_ref, upper), (lower_ref, lower))):
            store_registers(ref, lev, values)
            first = suffix(values, r0)[0]
            total = first + product[0] * chunk_inflow(steps, first, none)
            q_ref[lev + (k + 1) * LEV:lev + (k + 1) * LEV + 1, :] = total[0:1]

    copies = []
    for g in range(LEV // GROUP):
        for lev in range(g * GROUP, (g + 1) * GROUP):
            level(lev, lev % ABREAST)
        for i, (source, target) in enumerate(outs):
            part = pl.ds(g * GROUP, GROUP)
            copies.append(pltpu.make_async_copy(source.at[part], target.at[part], sems.at[g, i]))
            copies[-1].start()
    for copy in copies:
        copy.wait()


def split(x):
    high = x.astype(BF16).astype(F32)
    return high, x - high


def product_nt(a, b):
    return lax.dot_general(a, b, (((1,), (1,)), ((), ())), preferred_element_type=F32)


def state_kernel(recv_hbm, north_ref, up_ref, dn_ref, w1_hbm, w0_hbm, q1_ref,
                 send_ref, y_ref, flux_ref,
                 recv_ref, recv_sems, w1_ref, w0_ref, in_sems, x_ref, f1_ref, f0_ref, v_ref, e_ref, q_ref, t_ref, t2_ref, u_ref, p_ref, b_ref, term_ref, lhs_ref, mask_ref, hot_ref):
    is_top = top_flag()
    arrivals = [
        pltpu.make_async_copy(recv_hbm.at[pl.ds(b * 128, 128)], recv_ref.at[pl.ds(b * 128, 128)], recv_sems.at[b])
        for b in range(N_LAT)
    ]
    for arrival in arrivals:
        arrival.start()
    fetches = [
        pltpu.make_async_copy(source, target, in_sems.at[i])
        for i, (source, target) in enumerate(
            ((w1_hbm, w1_ref), (w0_hbm, w0_ref)))
    ]
    for fetch in fetches:
        fetch.start()
    for b in range(N_LAT):
        arrivals[b].wait()
        x_ref[:, b * 128:(b + 1) * 128] = recv_ref[b * 128:(b + 1) * 128, :].T

    def place(offset, n):
        cell = x_ref[offset + 36 + n:offset + 37 + n, :].astype(jnp.int32)
        return cell >> 7, cell & 127

    def make_terms(offset, n):
        parts = []
        for t in range(TR):
            value = x_ref[offset + 32 + 2 * n + t:offset + 33 + 2 * n + t, :]
            parts.append(split(value * x_ref[offset + n * LEV:offset + (n + 1) * LEV, :]))
        return parts

    for n in (1, 0):
        parts = make_terms(0, n)
        for t in range(TR):
            for p in range(2):
                term_ref[n, t, p] = parts[t][p]
        row, _ = place(0, n)
        later = row >= HALF
        row = jnp.where(later, row - HALF, row)
        mask_ref[n] = jnp.where(iota((HALF, SLOTS), 0) == row, 1.0, 0.0).astype(BF16)
        cell = recv_ref[:, 36 + n:37 + n].astype(jnp.int32)
        col = (cell & 127) + jnp.where(cell >= HALF * COLS, COLS, 0)
        hot_ref[n] = jnp.where(iota((SLOTS, 2 * COLS), 1) == col, 1.0, 0.0).astype(BF16)

    def deposit(g):
        for n in (1, 0):
            target = (f0_ref, f1_ref)[n]
            for i in range(GROUP):
                for t in range(TR):
                    for p in range(2):
                        at = ((i * TR + t) * 2 + p) * HALF
                        term = term_ref[n, t, p, g * GROUP + i:g * GROUP + i + 1, :]
                        term = jnp.broadcast_to(term, (16, SLOTS)).astype(BF16)
                        lhs_ref[n, at:at + HALF, :] = mask_ref[n] * jnp.concatenate([term] * 3, axis=0)
            out = jnp.dot(lhs_ref[n], hot_ref[n], preferred_element_type=F32)
            for i in range(GROUP):
                for t in range(TR):
                    at = (i * TR + t) * 2 * HALF
                    both = out[at:at + HALF] + out[at + HALF:at + 2 * HALF]
                    target[t * LEV + g * GROUP + i, TOP:TOP + HALF, :] = both[:, :COLS]
                    target[t * LEV + g * GROUP + i, TOP + HALF:END, :] = both[:, COLS:]

    edges = {}
    for side, offset in ((0, FIELDS), (1, 2 * FIELDS)):
        for n in (1, 0):
            rows = ((ROWS - 1, ROWS - 2), (0, 1))[side][:2 if n else 1]
            row, col = place(offset, n)
            hot = jnp.where(iota((COLS, SLOTS), 0) == col, 1.0, 0.0).astype(BF16)
            parts = make_terms(offset, n)
            stack = []
            for r in rows:
                hit = jnp.where(row == r, 1.0, 0.0)
                for t in range(TR):
                    for p in range(2):
                        stack.append((parts[t][p] * hit).astype(BF16))
            out = product_nt(jnp.concatenate(stack, axis=0), hot)
            for i in range(len(rows)):
                for t in range(TR):
                    at = (i * TR + t) * 2 * LEV
                    edges[side, n, i, t] = out[at:at + LEV] + out[at + LEV:at + 2 * LEV]

    for (side, n, i, t), value in edges.items():
        if n == 1:
            e_ref[side, i, t] = value
        if i == 0:
            where = iota((8, COLS), 0) == (7 if side == 0 else 0)
            at = 0 if side == 0 else END
            for lev in range(LEV):
                (f0_ref, f1_ref)[n][t * LEV + lev, at:at + 8, :] = jnp.where(where, value[lev:lev + 1, :], 0.0)
    for lev in range(LEV):
        v_ref[1, lev, TOP - 1:TOP, :] = up_ref[2, lev:lev + 1, :]
        v_ref[0, lev, TOP - 1:TOP, :] = up_ref[0, lev:lev + 1, :]
    low_north = jnp.maximum(up_ref[2], 0.0)
    low_south = jnp.minimum(up_ref[1], 0.0)
    high_north = jnp.maximum(dn_ref[0], 0.0)
    high_south = jnp.minimum(jnp.where(is_top, 0.0, north_ref[1, :, ROWS - 1, :]), 0.0)
    deposit(0)
    for fetch in fetches:
        fetch.wait()

    def edge_rows(lev, t):
        at = t * LEV + lev
        one = slice(lev, lev + 1)
        low, below = e_ref[0, 0, t, one, :], e_ref[0, 1, t, one, :]
        low = low + low_north[one] * (f1_ref[at, TOP:TOP + 1, :] - low) + low_south[one] * (low - below)
        high, above = e_ref[1, 0, t, one, :], e_ref[1, 1, t, one, :]
        high = high + high_north[one] * (above - high) + high_south[one] * (high - f1_ref[at, END - 1:END, :])
        row = iota((32, COLS), 0)
        return jnp.where(row == 0, high, jnp.where(row == 31, low, 0.0))

    none = jnp.zeros((8, 128), F32)
    below = jnp.zeros((32, COLS), F32)

    def transported(ref, n, lev, at):
        north = jnp.maximum(v_ref[n, lev, TOP:END, :], 0.0)
        south = jnp.minimum(v_ref[n, lev, TOP - 1:END - 1, :], 0.0)
        a = ref[at, TOP:END, :]
        return a + north * (ref[at, TOP + 1:END + 1, :] - a) + south * (a - ref[at, TOP - 1:END - 1, :])

    def latitude1(lev, slot):
        for n in range(STEPS):
            v_ref[n, lev, TOP:END, :] = masked_north(north_ref[n, lev], is_top)
        for t in range(TR):
            t_ref[slot + t] = jnp.concatenate([transported(f1_ref, 1, lev, t * LEV + lev), edge_rows(lev, t)], axis=0).T

    def longitude1(levels):
        ends, firsts = [], []
        for lev in levels:
            slot = TR * (lev % ABREAST)
            product, later = None, [None] * TR
            for m in BACKWARD:
                w = w1_ref[lev, register(m), :]
                r = 1.0 - w
                product = step(r, product)
                p_ref[lev % ABREAST, register(m), :] = product
                for t in range(TR):
                    later[t] = step(r, later[t], w * t_ref[slot + t, column(m), :])
                    t2_ref[slot + t, register(m), :] = later[t]
            ends.append(product)
            firsts += later
        of = [i for i in range(len(levels)) for _ in range(TR)]
        enter = chunk_inflows(chunk_ladders(ends), firsts, [none] * len(firsts), of)
        for i, lev in enumerate(levels):
            slot = TR * (lev % ABREAST)
            for m in range(CHUNK):
                product = p_ref[lev % ABREAST, register(m), :]
                for t in range(TR):
                    rest = t2_ref[slot + t, register(m), :] + product * enter[TR * i + t]
                    if m == 0:
                        at = t * LEV + lev
                        q_ref[at:at + 1, :] = rest[0:1]
                    u_ref[slot + t, column(m), :] = rest

    def latitude0(lev, slot):
        for t in range(TR):
            at = t * LEV + lev
            rest = u_ref[slot + t].T
            b_ref[slot + t, TOP:END, :] = f0_ref[at, TOP:END, :] + rest[0:ROWS]
            b_ref[slot + t, 0:TOP, :] = f0_ref[at, 0:TOP, :] + rest[120:128]
            b_ref[slot + t, END:PAD, :] = f0_ref[at, END:PAD, :] + rest[ROWS:ROWS + 8]
            if lev == 0:
                flux_ref[t] = f1_ref[at, TOP:END, :] + b_ref[slot + t, TOP:END, :]
            t_ref[slot + t] = jnp.concatenate([transported(b_ref, 0, lev, slot + t), below], axis=0).T

    def longitude0(levels):
        ends, firsts = [], []
        for lev in levels:
            slot = TR * (lev % ABREAST)
            product, later = None, [None] * TR
            for m in BACKWARD:
                w = w0_ref[lev, register(m), :]
                r = 1.0 - w
                product = step(r, product)
                for t in range(TR):
                    value = w * t_ref[slot + t, column(m), :]
                    y_ref[t * LEV + lev, register(m), :] = value
                    later[t] = step(r, later[t], value)
            ends.append(product)
            firsts += later
        of = [i for i in range(len(levels)) for _ in range(TR)]
        enter = chunk_inflows(chunk_ladders(ends), firsts, [none] * len(firsts), of)
        for i, lev in enumerate(levels):
            for t in range(TR):
                total = firsts[TR * i + t] + ends[i] * enter[TR * i + t]
                at = TR * LEV + t * LEV + lev
                q_ref[at:at + 1, :] = total[0:1]

    for g in range(LEV // GROUP):
        if g + 1 < LEV // GROUP:
            deposit(g + 1)
        levels = range(g * GROUP, (g + 1) * GROUP)
        for lev in levels:
            latitude1(lev, TR * (lev % ABREAST))
        longitude1(levels)
        for lev in levels:
            latitude0(lev, TR * (lev % ABREAST))
        longitude0(levels)
    q1 = q1_ref[...]
    gamma, gain0 = q1[3 * LEV:4 * LEV], q1[4 * LEV:]
    lane = iota((LEV, 128), 1)
    rows = []
    bases = [q_ref[i * LEV:(i + 1) * LEV, :] for i in range(4)] + [q1[LEV:2 * LEV], q1[0:LEV], q1[2 * LEV:3 * LEV]]
    riders = [(gain0, 65), (gain0, 35), (gamma, 96), (gamma, 64), (gamma, 32), (gain0, 5), (gain0, 96)]
    for i, (base, (rider, shift)) in enumerate(zip(bases, riders)):
        spare = (lane > ROWS) & (lane < 127) if i in (0, 1, 5) else lane >= ROWS
        rows.append(jnp.where(spare, pltpu.roll(rider, shift, 1), base))
    payload = jnp.concatenate(rows, axis=0)
    for j in range(N_LON):
        send_ref[j] = payload


def final_kernel(recv_ref, y_ref, here_ref, upper_ref, lower_ref, w0_ref, gain_ref, f_ref,
                 adj_hbm, flux_ref, adj_ref, sems, gamma_ref, gain0_ref, in1_ref, in0_ref, flow_ref, t_ref, u_ref, p_ref):
    me = lax.axis_index("lon")

    def part(j, i):
        return recv_ref[j, i * LEV:(i + 1) * LEV, :]

    lane = iota((LEV, 128), 1)

    def gamma(j):
        first, second, third = (pltpu.roll(part(j, 2 + i), 32 * (i + 1), 1) for i in range(3))
        return jnp.where(lane < 32, first, jnp.where(lane < 64, second, third))

    def gain0(j):
        pieces = [pltpu.roll(part(j, i), shift, 1) for i, shift in ((6, 32), (0, 63), (1, 93), (5, 123))]
        return jnp.where(lane < 32, pieces[0],
                         jnp.where(lane < 62, pieces[1], jnp.where(lane < 92, pieces[2], pieces[3])))

    for j in range(N_LON):
        gamma_ref[j] = gamma(j)
        gain0_ref[j] = gain0(j)

    def both(x):
        return jnp.concatenate([x, x], axis=0)

    pair = (TR * LEV, 128)
    gain = jnp.ones((LEV, 128), F32)
    rest = jnp.zeros(pair, F32)
    for j in range(N_LON - 1, -1, -1):
        g = part(j, 5)
        rest = both(g) * rest + recv_ref[j, 0:TR * LEV, :]
        gain = g * gain
    inflow = rest * both(1.0 / (1.0 - gain))
    gain = jnp.ones((LEV, 128), F32)
    rest = jnp.zeros(pair, F32)
    for j in range(N_LON - 1, -1, -1):
        in1_ref[j] = inflow
        total = recv_ref[j, TR * LEV:2 * TR * LEV, :] + both(part(j, 4)) * inflow
        total = total + both(part(j, 6)) * row_ahead(inflow) + both(gamma_ref[j]) * row_behind(inflow)
        in0_ref[j] = total
        inflow = both(part(j, 5)) * inflow + recv_ref[j, 0:TR * LEV, :]
        g = gain0_ref[j]
        rest = both(g) * rest + total
        gain = g * gain
    inflow = rest * both(1.0 / (1.0 - gain))
    for j in range(N_LON - 1, -1, -1):
        total = in0_ref[j]
        in0_ref[j] = inflow
        inflow = both(gain0_ref[j]) * inflow + total
    mine = in1_ref[me]
    flow_ref[0] = mine
    flow_ref[1] = row_ahead(mine)
    flow_ref[2] = row_behind(mine)
    flow_ref[3] = in0_ref[me]

    for t in range(TR):
        flow = flow_ref[0, t * LEV:t * LEV + 1, :]
        for m in range(CHUNK):
            t_ref[t, column(m), :] = gain_ref[0, register(m), :] * flow
        flux_ref[t] = f_ref[t] + t_ref[t].T[0:ROWS]

    def longitude0(levels):
        ends, firsts, inflows = [], [], []
        for lev in levels:
            product, later = None, [None] * TR
            flows = [[flow_ref[i, t * LEV + lev:t * LEV + lev + 1, :] for i in range(4)] for t in range(TR)]
            for m in BACKWARD:
                r = 1.0 - w0_ref[lev, register(m), :]
                product = step(r, product)
                p_ref[lev % FINAL_ABREAST, register(m), :] = product
                here, upper, lower = (ref[lev, register(m), :] for ref in (here_ref, upper_ref, lower_ref))
                for t in range(TR):
                    at = t * LEV + lev
                    value = y_ref[at, register(m), :] + here * flows[t][0] + upper * flows[t][1] + lower * flows[t][2]
                    later[t] = step(r, later[t], value)
                    u_ref[TR * (lev % FINAL_ABREAST) + t, register(m), :] = later[t]
            ends.append(product)
            firsts += later
            inflows += [flows[t][3] for t in range(TR)]
        of = [i for i in range(len(levels)) for _ in range(TR)]
        enter = chunk_inflows(chunk_ladders(ends), firsts, inflows, of)
        for i, lev in enumerate(levels):
            for t in range(TR):
                slot = TR * (lev % FINAL_ABREAST) + t
                for m in range(CHUNK):
                    value = u_ref[slot, register(m), :]
                    value = value + p_ref[lev % FINAL_ABREAST, register(m), :] * enter[TR * i + t]
                    t_ref[slot, column(m), :] = value
                adj_ref[t, lev] = t_ref[slot].T[0:ROWS]

    copies = []
    for g in range(LEV // GROUP):
        longitude0(range(g * GROUP, (g + 1) * GROUP))
        for t in range(TR):
            part_of = pl.ds(g * GROUP, GROUP)
            copies.append(pltpu.make_async_copy(adj_ref.at[t, part_of], adj_hbm.at[t, part_of], sems.at[g, t]))
            copies[-1].start()
    for copy in copies:
        copy.wait()


def whole(shape):
    return pl.BlockSpec(shape, lambda i: (0,) * len(shape))


def in_hbm(*arrays):
    return [pltpu.with_memory_space_constraint(x, pltpu.HBM) for x in arrays]


ANYWHERE = pl.BlockSpec(memory_space=pltpu.HBM)


def call(kernel, steps, outs, in_specs, scratch, name, mega, cost=None):
    return pl.pallas_call(
        kernel,
        grid=(steps,),
        out_shape=[pltpu.HBM(s, F32) if hbm else jax.ShapeDtypeStruct(s, F32) for s, _, hbm in outs],
        in_specs=in_specs,
        out_specs=[whole(s) if spec is None else spec for s, spec, _ in outs],
        scratch_shapes=[pltpu.VMEM(*s) if isinstance(s, tuple) else s for s in scratch],
        compiler_params=pltpu.CompilerParams(vmem_limit_bytes=mega * MEGA),
        cost_estimate=cost,
        name=name,
    )


def shards(east, north, kernels, departures, cells, counts):
    send, up, dn = call(
        pack_kernel, 1,
        [((SLOTS, 128), ANYWHERE, True), ((4, LEV, COLS), None, False), ((2, LEV, COLS), None, False)],
        [ANYWHERE] * 6,
        [(kernels.shape, F32), (departures.shape, F32), (cells.shape, jnp.int32), (counts.shape, jnp.int32),
         ((STEPS, LEV, 8, COLS), F32), ((LEV, 8, COLS), F32), ((LEV, 8, COLS), F32), ((LEV, 8, COLS), F32),
         ((FIELDS, SLOTS), F32), ((SLOTS, 128), F32), pltpu.SemaphoreType.DMA((8,)),
         pltpu.SemaphoreType.DMA((N_LAT,))],
        "pack", 8,
    )(*in_hbm(kernels, departures, cells, counts, north, east))
    recv = lax.all_to_all(send.reshape(128, 8, 128), ("lat", "lon"), split_axis=0, concat_axis=0, tiled=True)
    up = lax.ppermute(up, "lat", [(i, i + 1) for i in range(N_LAT - 1)])
    dn = lax.ppermute(dn, "lat", [(i + 1, i) for i in range(N_LAT - 1)])
    turned = (LEV, 128, 128)
    w1, w0, here, upper, lower, gain, q1 = call(
        coef_kernel, 1,
        [(turned, ANYWHERE, True)] * 5 + [((1, 128, 128), None, True), ((COEF, 128), None, False)],
        [whole(east.shape), pl.BlockSpec((1, LEV, ROWS, COLS), lambda i: (0, 0, 0, 0)), whole(up.shape), whole(dn.shape)],
        [(turned, F32)] * 5 + [pltpu.SemaphoreType.DMA((LEV // GROUP, 5)),
         ((LEV, 32, COLS), F32), ((LEV, 32, COLS), F32), ((ABREAST, 3, 128, 128), F32)],
        "coef", 16, pl.CostEstimate(flops=2 * 10**8, transcendentals=0, bytes_accessed=6 * 10**7),
    )(east, north, up, dn)
    tiles = (TR * LEV, 128, 128)
    send2, y, f = call(
        state_kernel, 1,
        [((N_LON, PAYLOAD, 128), None, False), (tiles, None, False), ((TR, ROWS, COLS), None, False)],
        [ANYWHERE, whole(north.shape), whole(up.shape), whole(dn.shape)] + [ANYWHERE] * 2 + [whole(q1.shape)],
        [((SLOTS, 128), F32), pltpu.SemaphoreType.DMA((N_LAT,))] + [(turned, F32)] * 2 + [pltpu.SemaphoreType.DMA((2,)),
         ((128, SLOTS), F32), ((TR * LEV, PAD, COLS), F32), ((TR * LEV, PAD, COLS), F32),
         ((STEPS, LEV, PAD, COLS), F32), ((2, 2, TR, LEV, COLS), F32), ((REST, 128), F32),
         ((TR * ABREAST, 128, 128), F32), ((TR * ABREAST, 128, 128), F32), ((TR * ABREAST, 128, 128), F32),
         ((ABREAST, 128, 128), F32), ((TR * ABREAST, PAD, COLS), F32), ((STEPS, TR, 2, LEV, SLOTS), F32), ((2, 16 * HALF, SLOTS), BF16), ((STEPS, HALF, SLOTS), BF16),
         ((STEPS, SLOTS, 2 * COLS), BF16)],
        "state", 32,
    )(*in_hbm(recv.reshape(SLOTS, 128)), north, up, dn, *in_hbm(w1, w0), q1)
    recv2 = lax.all_to_all(send2, "lon", split_axis=0, concat_axis=0, tiled=True)
    adjoint, flux = call(
        final_kernel, 1,
        [((TR, LEV, ROWS, COLS), ANYWHERE, True), ((TR, ROWS, COLS), None, True)],
        [whole(recv2.shape), whole(tiles)] + [whole(turned)] * 4 + [whole(gain.shape), whole(f.shape)],
        [((TR, LEV, ROWS, COLS), F32), pltpu.SemaphoreType.DMA((LEV // GROUP, TR)), ((N_LON, LEV, 128), F32),
         ((N_LON, LEV, 128), F32), ((N_LON, TR * LEV, 128), F32), ((N_LON, TR * LEV, 128), F32), ((4, TR * LEV, 128), F32),
         ((TR * FINAL_ABREAST, 128, 128), F32), ((TR * FINAL_ABREAST, 128, 128), F32),
         ((FINAL_ABREAST, 128, 128), F32)],
        "final", 24,
    )(recv2, y, here, upper, lower, w0, gain, f)
    return adjoint, flux


def solution(mesh):
    return jax.shard_map(
        shards,
        mesh=mesh,
        in_specs=(
            P(None, None, "lat", "lon"),
            P(None, None, "lat", "lon"),
            P(None, None, ("lat", "lon")),
            P(None, None, ("lat", "lon")),
            P(None, ("lat", "lon")),
            P(None, ("lat", "lon")),
        ),
        out_specs=(P(None, None, "lat", "lon"), P(None, "lat", "lon")),
        check_vma=False,
    )
```
